512 devices in a mesh: expert: 64 (over x, z), tensor: 8 (over y, core).
Axes of the slice: x: 4, y: 4, z: 16, core: 2. Of those that a mesh axis runs over, the one named last changes fastest.
Arguments:
- tokens: bfloat16 [1024, 7168], P('expert', 'tensor'), may hold values from -6 to 6
- expert_ids: int32 [1024, 8], P('expert'), may hold values from 0 to 31, as said below
- route_weights: float32 [1024, 8], P('expert'), may hold values from 0.05 to 1
- gate_weight: bfloat16 [64, 512, 7168], P('expert', 'tensor'), may hold values from -0.0625 to 0.0625
- up_weight: bfloat16 [64, 512, 7168], P('expert', 'tensor'), may hold values from -0.0625 to 0.0625
- down_weight: bfloat16 [64, 512, 7168], P('expert', 'tensor'), may hold values from -0.1875 to 0.1875
Outputs:
- mixed: bfloat16 [1024, 7168], P('expert', 'tensor')
The draws below stay inside these ranges and needn't reach their ends.
Inputs may be any that keep to these rules, and one draw needn't show every extreme that they name: `expert_ids`: each row holds 8 different experts. One expert, the same for all tokens, is named by exactly 4 of the 16 tokens of every block of 16 consecutive tokens; every other expert by at most 4 tokens of a block.
All inputs are finite; a program needn't handle non-finite values.
Results may differ from the reference program's by a relative error of at most 0.015.
Values may be sent and summed in bfloat16 or wider, within the bound.
No kernel may reach another device: no remote copies, remote signals or barrier semaphores. Data moves between devices by JAX's collectives and lax.ppermute only.
A program may use at most 64 MiB of HBM per device.

```python
import math
import jax
import jax.numpy as jnp
from jax import lax

D = 7168
TOP = 8
FF = 1024
TOK_DEV = 16
EXPERTS = 32
TOKENS = 1024
CAP = 4
N_TENSOR = 8


def draw_expert_ids(key, part):
    hot_expert = jax.random.randint(jax.random.fold_in(key, 7), (), 0, EXPERTS)
    block_keys = jax.random.split(jax.random.fold_in(key, 11), TOKENS // TOK_DEV)
    column = jnp.arange(TOP, dtype=jnp.int32)

    def one_block(block_key):
        key_order = jax.random.fold_in(block_key, 1)
        key_others = jax.random.fold_in(block_key, 2)
        key_columns = jax.random.fold_in(block_key, 3)
        position = jax.random.permutation(key_order, TOK_DEV).astype(jnp.int32)
        others = jax.random.permutation(key_others, EXPERTS - 1).astype(jnp.int32)
        others = others + (others >= hot_expert).astype(jnp.int32)
        is_hot = position < CAP
        offset = jnp.where(is_hot, position * (TOP - 1), CAP * (TOP - 1) + (position - CAP) * TOP)
        shifted = is_hot.astype(jnp.int32)
        index_table = jnp.mod(offset[:, None] + column[None, :] - shifted[:, None], EXPERTS - 1)
        rows = others[index_table]
        rows = jnp.where(is_hot[:, None] & (column[None, :] == 0), hot_expert, rows)
        scores = jax.random.randint(key_columns, (TOK_DEV, TOP), 0, 1 << 20) * TOP + column[None, :]
        order = jnp.argsort(scores, axis=1)
        return jnp.take_along_axis(rows, order, axis=1)
    result = jax.vmap(one_block)(block_keys)
    return result.reshape(TOKENS, TOP).astype(jnp.int32)


def block_scale(stream_key, dims, pieces, smallest, top_value):
    level, own = 1.0, jax.random.fold_in(stream_key, 6)
    for dim, parts in pieces:
        heights = jnp.exp(jax.random.uniform(jax.random.fold_in(own, dim), (parts,), jnp.float32, smallest / len(pieces), top_value / len(pieces)))
        level = level * jnp.repeat(heights, dims[dim] // parts).reshape([-1 if axis == dim else 1 for axis in range(len(dims))])
    return level


def noise(stream_key, dims, width, limit, cuts=(), held_as=jnp.bfloat16):
    values = jax.random.normal(stream_key, dims, jnp.float32) * width
    if len(cuts) > 0:
        values = block_scale(stream_key, dims, cuts, -0.22, 0.18) * values
    return jnp.clip(values, min=-limit, max=limit).astype(held_as)


def setup_inputs(seed: int = 0) -> dict:
    key_of = jax.random.split(jax.random.key(seed), 7)
    return {
        "tokens": noise(key_of[0], (TOKENS, D), 1.0, 6.0, ((0, 64), (1, 8))),
        "expert_ids": draw_expert_ids(jax.random.fold_in(key_of[6], 71), 0),
        "route_weights": jnp.clip(jnp.exp(math.log(1.0) - 2.9957323 * jax.random.uniform(key_of[2], (TOKENS, TOP), jnp.float32) ** block_scale(key_of[2], (TOKENS, TOP), ((0, 64),), -0.2, 0.2)), 0.05, 1.0),
        "gate_weight": noise(key_of[3], (2 * EXPERTS, FF // 2, D), D ** -0.5, 0.0625, ((0, 64), (1, 8))),
        "up_weight": noise(key_of[4], (2 * EXPERTS, FF // 2, D), D ** -0.5, 0.0625, ((0, 64), (1, 8))),
        "down_weight": noise(key_of[5], (2 * EXPERTS, FF // 2, D), FF ** -0.5, 0.1875, ((0, 64), (1, 8))),
    }


def reference(tokens, expert_ids, route_weights, gate_weight, up_weight, down_weight):
    block_count = TOKENS // TOK_DEV
    slot_count = block_count * CAP
    unit_count = FF // (2 * N_TENSOR)
    expert_range = jnp.arange(EXPERTS, dtype=jnp.int32)
    onehot = jnp.sum((expert_ids[:, :, None] == expert_range[None, None, :]).astype(jnp.int32), axis=1)
    onehot_blocks = onehot.reshape(block_count, TOK_DEV, EXPERTS)
    earlier_count = (jnp.cumsum(onehot_blocks, axis=1) - onehot_blocks).reshape(TOKENS, EXPERTS)
    slot_rank = jnp.take_along_axis(earlier_count, expert_ids, axis=1)
    token_range = jnp.arange(TOKENS, dtype=jnp.int32)
    slot_index = (token_range // TOK_DEV)[:, None] * CAP + slot_rank
    token_table = jnp.full((EXPERTS, slot_count), TOKENS, dtype=jnp.int32)
    token_table = token_table.at[expert_ids, slot_index].set(jnp.broadcast_to(token_range[:, None], expert_ids.shape))
    padded = jnp.concatenate([tokens, jnp.zeros((1, D), jnp.bfloat16)], axis=0)

    def run_expert(expert):
        expert_rows = padded[token_table[expert]]
        halves = []
        for half in range(2):
            entry = 2 * expert + half
            gate_act = jnp.dot(expert_rows, gate_weight[entry].T, preferred_element_type=jnp.float32)
            up_act = jnp.dot(expert_rows, up_weight[entry].T, preferred_element_type=jnp.float32)
            hidden = (jax.nn.silu(gate_act) * up_act).astype(jnp.bfloat16)
            hidden_groups = hidden.reshape(slot_count, N_TENSOR, unit_count).astype(jnp.float32)
            down_groups = down_weight[entry].reshape(N_TENSOR, unit_count, D).astype(jnp.float32)
            group_terms = jnp.einsum("rgf,gfd->grd", hidden_groups, down_groups).astype(jnp.bfloat16)
            group_terms = lax.optimization_barrier(group_terms)
            halves.append(jnp.sum(group_terms.astype(jnp.float32), axis=0).astype(jnp.bfloat16))
        return jnp.stack(halves, axis=0)

    half_out = lax.map(run_expert, expert_range)
    picked = half_out[expert_ids, 0, slot_index].astype(jnp.float32) + half_out[expert_ids, 1, slot_index].astype(jnp.float32)
    mixed = jnp.sum(route_weights[:, :, None] * picked, axis=1)
    return mixed.astype(jnp.bfloat16)
```

```python
import jax
import jax.numpy as jnp
from jax import lax
from jax.experimental import pallas as pl
from jax.experimental.pallas import tpu as pltpu
from jax.sharding import PartitionSpec as P

F32 = jnp.float32
BF16 = jnp.bfloat16


def slot_onehot(ids, lanes, capacity, copies):
    tok_count, per_token = ids.shape
    lane = lax.broadcasted_iota(jnp.int32, (tok_count, lanes), 1)
    expert = lane // (capacity * copies)
    hit = jnp.zeros((tok_count, lanes), F32)
    for j in range(per_token):
        hit = hit + jnp.where(ids[:, j : j + 1] == expert, 1.0, 0.0)
    row = lax.broadcasted_iota(jnp.int32, (tok_count, tok_count), 0)
    col = lax.broadcasted_iota(jnp.int32, (tok_count, tok_count), 1)
    lower = jnp.where(col < row, 1.0, 0.0).astype(BF16)
    earlier = jnp.dot(lower, hit.astype(BF16), preferred_element_type=F32)
    slot = (lane % capacity).astype(F32)
    return jnp.where((hit > 0.5) & (earlier == slot), 1.0, 0.0), expert


def pack_kernel(capacity, copies, ids_ref, tok_ref, out_ref):
    lanes = out_ref.shape[0]
    select, _ = slot_onehot(ids_ref[...], lanes, capacity, copies)
    out_ref[...] = lax.dot_general(
        select.astype(BF16), tok_ref[...], (((0,), (0,)), ((), ())), preferred_element_type=F32
    ).astype(BF16)


def mix_kernel(capacity, copies, ids_ref, route_ref, mix_ref):
    lanes = mix_ref.shape[1]
    ids = ids_ref[...]
    route = route_ref[...]
    select, expert = slot_onehot(ids, lanes, capacity, copies)
    weight = jnp.zeros(select.shape, F32)
    for j in range(ids.shape[1]):
        weight = weight + jnp.where(ids[:, j : j + 1] == expert, route[:, j : j + 1], 0.0)
    mix_ref[...] = select * weight


def combine_kernel(mix_ref, rows_ref, out_ref):
    mix = mix_ref[...]
    high = mix.astype(BF16)
    low = (mix - high.astype(F32)).astype(BF16)
    rows = rows_ref[...]
    total = jnp.dot(high, rows, preferred_element_type=F32)
    total = total + jnp.dot(low, rows, preferred_element_type=F32)
    out_ref[...] = total.astype(BF16)


CORES = 2
VMEM_BYTES = 16 * 2**20
SHIFTS = [(0, 0), (1, 0), (1, 1), (3, 0), (3, 1), (2, 0), (2, 1), (0, 1)]


def moved_by(index, groups, ring, core, sign=1):
    rings = groups // CORES
    place = lax.rem(index // CORES + sign * ring + rings, rings)
    return place * CORES + lax.rem(lax.rem(index, CORES) + core, CORES)


def shift_pairs(groups, ring, core):
    rings = groups // CORES
    return [
        (i, (i // CORES + ring) % rings * CORES + (i + core) % CORES) for i in range(groups)
    ]


def cut_kernel(groups, width, gate_ref, up_ref, *outs):
    me = lax.axis_index("tensor")
    units = gate_ref.shape[0]
    for out, shift in zip(outs, SHIFTS):
        target = moved_by(me, groups, *shift)
        cols = pl.ds(pl.multiple_of(target * width, 128), width)
        out[:units, :] = gate_ref[:, cols]
        out[units:, :] = up_ref[:, cols]


def cut_columns(gate, up, width):
    groups = gate.shape[1] // width
    shape = jax.ShapeDtypeStruct((2 * gate.shape[0], width), BF16)
    first, *rest = pl.pallas_call(
        lambda *refs: cut_kernel(groups, width, *refs),
        out_shape=[shape] * groups,
        compiler_params=pltpu.CompilerParams(vmem_limit_bytes=VMEM_BYTES),
        name="cut",
    )(gate, up)
    return first, rest


def up_kernel(rows_ref, *refs):
    *blocks, out_ref = refs
    groups = len(blocks)
    me = lax.axis_index("tensor")
    rows = rows_ref[...]
    for block, shift in zip(blocks, SHIFTS):
        source = moved_by(me, groups, *shift, sign=-1)
        out_ref[source] = lax.dot_general(
            block[...], rows, (((1,), (1,)), ((), ())), preferred_element_type=F32
        ).astype(BF16)


def hidden_kernel(partial_ref, out_ref):
    groups, units, _ = out_ref.shape
    act = partial_ref[0].astype(F32)
    for g in range(1, groups):
        act = act + partial_ref[g].astype(F32)
    gate, up = act[:units], act[units:]
    hidden = (jax.nn.silu(gate) * up).astype(BF16)
    for g in range(groups):
        out_ref[g] = hidden


def chip_cut_kernel(wide, weight_ref, *outs):
    rings = len(outs)
    chip = lax.axis_index("tensor") // CORES
    for ring, out in enumerate(outs):
        target = lax.rem(chip + ring, rings)
        out[...] = weight_ref[:, pl.ds(pl.multiple_of(target * wide, 128), wide)]


def core_cut_kernel(*refs):
    *blocks, near_ref, far_ref = refs
    core = lax.rem(lax.axis_index("tensor"), CORES)
    units = blocks[0].shape[0]
    width = near_ref.shape[1]
    for ring, block in enumerate(blocks):
        rows = pl.ds(ring * units, units)
        near_ref[rows, :] = block[:, pl.ds(pl.multiple_of(core * width, 128), width)]
        far_ref[rows, :] = block[:, pl.ds(pl.multiple_of((1 - core) * width, 128), width)]


def down_columns(weight, width, groups):
    units = weight.shape[0]
    rings, wide = groups // CORES, CORES * width
    first, *rest = pl.pallas_call(
        lambda *refs: chip_cut_kernel(wide, *refs),
        out_shape=[jax.ShapeDtypeStruct((units, wide), BF16)] * rings,
        compiler_params=pltpu.CompilerParams(vmem_limit_bytes=VMEM_BYTES),
        name="chip_cut",
    )(weight)
    rest = [
        lax.ppermute(block, "tensor", shift_pairs(groups, ring + 1, 0))
        for ring, block in enumerate(rest)
    ]
    near, far = pl.pallas_call(
        core_cut_kernel,
        out_shape=[jax.ShapeDtypeStruct((rings * units, width), BF16)] * 2,
        compiler_params=pltpu.CompilerParams(vmem_limit_bytes=VMEM_BYTES),
        name="core_cut",
    )(first, *rest)
    return near, lax.ppermute(far, "tensor", shift_pairs(groups, 0, 1))


def down_kernel(hidden_ref, near_ref, far_ref, out_ref, held):
    groups, units, _ = hidden_ref.shape
    me = lax.axis_index("tensor")
    for core in range(CORES):
        for ring in range(groups // CORES):
            source = moved_by(me, groups, ring, core, sign=-1)
            held[core, pl.ds(ring * units, units), :] = hidden_ref[source]
    dims = (((0,), (0,)), ((), ()))
    total = lax.dot_general(held[0], near_ref[...], dims, preferred_element_type=F32)
    total = total + lax.dot_general(held[1], far_ref[...], dims, preferred_element_type=F32)
    out_ref[...] = total.astype(BF16)


def body(tokens, expert_ids, route_weights, gate_weight, up_weight, down_weight):
    devices_wide = lax.axis_size("expert")
    groups = lax.axis_size("tensor")
    experts = devices_wide // 2
    tok_count, per_token = expert_ids.shape
    width = tokens.shape[1]
    units = gate_weight.shape[1]
    capacity = min(tok_count, tok_count * per_token // experts)
    arrived_count = devices_wide * capacity

    packed = pl.pallas_call(
        lambda *refs: pack_kernel(capacity, 2, *refs),
        out_shape=jax.ShapeDtypeStruct((arrived_count, width), BF16),
        compiler_params=pltpu.CompilerParams(vmem_limit_bytes=VMEM_BYTES),
        name="pack",
    )(expert_ids, tokens)
    mix = pl.pallas_call(
        lambda *refs: mix_kernel(capacity, 2, *refs),
        out_shape=jax.ShapeDtypeStruct((tok_count, arrived_count), F32),
        compiler_params=pltpu.CompilerParams(vmem_limit_bytes=VMEM_BYTES),
        name="mix",
    )(expert_ids, route_weights)

    keep, others = cut_columns(gate_weight[0], up_weight[0], width)
    moved = [
        lax.ppermute(block, "tensor", shift_pairs(groups, *shift))
        for block, shift in zip(others, SHIFTS[1:])
    ]
    arrived = lax.all_to_all(
        packed.reshape(devices_wide, capacity, width), "expert", 0, 0, tiled=True
    ).reshape(arrived_count, width)
    down_near, down_far = down_columns(down_weight[0], width, groups)

    partial = pl.pallas_call(
        up_kernel,
        out_shape=jax.ShapeDtypeStruct((groups, 2 * units, arrived_count), BF16),
        compiler_params=pltpu.CompilerParams(vmem_limit_bytes=VMEM_BYTES),
        name="gate_up",
    )(arrived, keep, *moved)
    partial = lax.all_to_all(partial, "tensor", 0, 0, tiled=True)
    hidden = pl.pallas_call(
        hidden_kernel,
        out_shape=jax.ShapeDtypeStruct((groups, units, arrived_count), BF16),
        compiler_params=pltpu.CompilerParams(vmem_limit_bytes=VMEM_BYTES),
        name="hidden",
    )(partial)
    hidden = lax.all_to_all(hidden, "tensor", 0, 0, tiled=True)
    half_out = pl.pallas_call(
        down_kernel,
        out_shape=jax.ShapeDtypeStruct((arrived_count, width), BF16),
        scratch_shapes=[pltpu.VMEM((2, groups // 2 * units, arrived_count), BF16)],
        compiler_params=pltpu.CompilerParams(vmem_limit_bytes=VMEM_BYTES),
        name="down",
    )(hidden, down_near, down_far)
    returned = lax.all_to_all(
        half_out.reshape(devices_wide, capacity, width), "expert", 0, 0, tiled=True
    ).reshape(arrived_count, width)
    return pl.pallas_call(
        combine_kernel,
        out_shape=jax.ShapeDtypeStruct((tok_count, width), BF16),
        compiler_params=pltpu.CompilerParams(vmem_limit_bytes=VMEM_BYTES),
        name="combine",
    )(mix, returned)


def solution(mesh):
    placed = (
        P("expert", "tensor"),
        P("expert", None),
        P("expert", None),
        P("expert", "tensor", None),
        P("expert", "tensor", None),
        P("expert", "tensor", None),
    )
    return jax.shard_map(
        body, mesh=mesh, in_specs=placed, out_specs=P("expert", "tensor"), check_vma=False
    )
```

```python
import jax
import jax.numpy as jnp
from jax import lax
from jax.experimental import pallas as pl
from jax.experimental.pallas import tpu as pltpu
from jax.sharding import PartitionSpec as P

F32 = jnp.float32
BF16 = jnp.bfloat16


def slot_onehot(ids, lanes, capacity, copies):
    tok_count, per_token = ids.shape
    lane = lax.broadcasted_iota(jnp.int32, (tok_count, lanes), 1)
    expert = lane // (capacity * copies)
    hit = jnp.zeros((tok_count, lanes), F32)
    for j in range(per_token):
        hit = hit + jnp.where(ids[:, j : j + 1] == expert, 1.0, 0.0)
    row = lax.broadcasted_iota(jnp.int32, (tok_count, tok_count), 0)
    col = lax.broadcasted_iota(jnp.int32, (tok_count, tok_count), 1)
    lower = jnp.where(col < row, 1.0, 0.0).astype(BF16)
    earlier = jnp.dot(lower, hit.astype(BF16), preferred_element_type=F32)
    slot = (lane % capacity).astype(F32)
    return jnp.where((hit > 0.5) & (earlier == slot), 1.0, 0.0), expert


def pack_kernel(capacity, copies, ids_ref, tok_ref, out_ref):
    lanes = out_ref.shape[0]
    select, _ = slot_onehot(ids_ref[...], lanes, capacity, copies)
    out_ref[...] = lax.dot_general(
        select.astype(BF16), tok_ref[...], (((0,), (0,)), ((), ())), preferred_element_type=F32
    ).astype(BF16)


def mix_kernel(capacity, copies, ids_ref, route_ref, mix_ref):
    lanes = mix_ref.shape[1]
    ids = ids_ref[...]
    route = route_ref[...]
    select, expert = slot_onehot(ids, lanes, capacity, copies)
    weight = jnp.zeros(select.shape, F32)
    for j in range(ids.shape[1]):
        weight = weight + jnp.where(ids[:, j : j + 1] == expert, route[:, j : j + 1], 0.0)
    mix_ref[...] = select * weight


def combine_kernel(mix_ref, rows_ref, out_ref):
    mix = mix_ref[...]
    high = mix.astype(BF16)
    low = (mix - high.astype(F32)).astype(BF16)
    rows = rows_ref[...]
    total = jnp.dot(high, rows, preferred_element_type=F32)
    total = total + jnp.dot(low, rows, preferred_element_type=F32)
    out_ref[...] = total.astype(BF16)


CORES = 2
VMEM_BYTES = 16 * 2**20


def moved_by(index, groups, ring, core, sign=1):
    rings = groups // CORES
    place = lax.rem(index // CORES + sign * ring + rings, rings)
    return place * CORES + lax.rem(lax.rem(index, CORES) + core, CORES)


def shift_pairs(groups, ring, core):
    rings = groups // CORES
    return [
        (i, (i // CORES + ring) % rings * CORES + (i + core) % CORES) for i in range(groups)
    ]


def cut_kernel(wide, gate_ref, up_ref, *outs):
    rings = len(outs)
    units = gate_ref.shape[0]
    chip = lax.axis_index("tensor") // CORES
    for ring, out in enumerate(outs):
        target = lax.rem(chip + ring, rings)
        cols = pl.ds(pl.multiple_of(target * wide, 128), wide)
        out[:units, :] = gate_ref[:, cols]
        out[units:, :] = up_ref[:, cols]


def chip_blocks(gate, up, width, groups):
    wide, rings = CORES * width, groups // CORES
    shape = jax.ShapeDtypeStruct((2 * gate.shape[0], wide), BF16)
    first, *rest = pl.pallas_call(
        lambda *refs: cut_kernel(wide, *refs),
        out_shape=[shape] * rings,
        compiler_params=pltpu.CompilerParams(vmem_limit_bytes=VMEM_BYTES),
        name="cut",
    )(gate, up)
    return [first] + [
        lax.ppermute(block, "tensor", shift_pairs(groups, ring + 1, 0))
        for ring, block in enumerate(rest)
    ]


def half_product(block_ref, rows_ref, half):
    width = rows_ref.shape[1]
    cols = pl.ds(pl.multiple_of(half * width, 128), width)
    return lax.dot_general(
        block_ref[:, cols], rows_ref[...], (((1,), (1,)), ((), ())), preferred_element_type=F32
    )


def near_kernel(rows_ref, *refs):
    *blocks, out_ref = refs
    chip, core = lax.axis_index("tensor") // CORES, lax.rem(lax.axis_index("tensor"), CORES)
    for ring, block in enumerate(blocks):
        source = lax.rem(chip - ring + len(blocks), len(blocks))
        out_ref[source] = half_product(block, rows_ref, core)


def far_kernel(rows_ref, near_ref, *refs):
    *blocks, out_ref = refs
    chip, core = lax.axis_index("tensor") // CORES, lax.rem(lax.axis_index("tensor"), CORES)
    for ring, block in enumerate(blocks):
        source = lax.rem(chip - ring + len(blocks), len(blocks))
        out_ref[source] = (near_ref[source] + half_product(block, rows_ref, 1 - core)).astype(BF16)


def hidden_kernel(partial_ref, out_ref):
    groups, units, _ = out_ref.shape
    act = partial_ref[0].astype(F32)
    for g in range(1, partial_ref.shape[0]):
        act = act + partial_ref[g].astype(F32)
    gate, up = act[:units], act[units:]
    hidden = (jax.nn.silu(gate) * up).astype(BF16)
    for g in range(groups):
        out_ref[g] = hidden


def chip_cut_kernel(wide, weight_ref, *outs):
    rings = len(outs)
    chip = lax.axis_index("tensor") // CORES
    for ring, out in enumerate(outs):
        target = lax.rem(chip + ring, rings)
        out[...] = weight_ref[:, pl.ds(pl.multiple_of(target * wide, 128), wide)]


def core_cut_kernel(*refs):
    *blocks, near_ref, far_ref = refs
    core = lax.rem(lax.axis_index("tensor"), CORES)
    units = blocks[0].shape[0]
    width = near_ref.shape[1]
    for ring, block in enumerate(blocks):
        rows = pl.ds(ring * units, units)
        near_ref[rows, :] = block[:, pl.ds(pl.multiple_of(core * width, 128), width)]
        far_ref[rows, :] = block[:, pl.ds(pl.multiple_of((1 - core) * width, 128), width)]


def down_columns(weight, width, groups):
    units = weight.shape[0]
    rings, wide = groups // CORES, CORES * width
    first, *rest = pl.pallas_call(
        lambda *refs: chip_cut_kernel(wide, *refs),
        out_shape=[jax.ShapeDtypeStruct((units, wide), BF16)] * rings,
        compiler_params=pltpu.CompilerParams(vmem_limit_bytes=VMEM_BYTES),
        name="chip_cut",
    )(weight)
    for ring in range(1, rings):
        rest[ring - 1] = lax.ppermute(
            rest[ring - 1], "tensor", shift_pairs(groups, ring, 0)
        )
    near, far = pl.pallas_call(
        core_cut_kernel,
        out_shape=[jax.ShapeDtypeStruct((rings * units, width), BF16)] * 2,
        compiler_params=pltpu.CompilerParams(vmem_limit_bytes=VMEM_BYTES),
        name="core_cut",
    )(first, *rest)
    return near, lax.ppermute(far, "tensor", shift_pairs(groups, 0, 1))


def down_kernel(hidden_ref, near_ref, far_ref, out_ref, held):
    groups, units, _ = hidden_ref.shape
    me = lax.axis_index("tensor")
    for core in range(CORES):
        for ring in range(groups // CORES):
            source = moved_by(me, groups, ring, core, sign=-1)
            held[core, pl.ds(ring * units, units), :] = hidden_ref[source]
    dims = (((0,), (0,)), ((), ()))
    total = lax.dot_general(held[0], near_ref[...], dims, preferred_element_type=F32)
    total = total + lax.dot_general(held[1], far_ref[...], dims, preferred_element_type=F32)
    out_ref[...] = total.astype(BF16)


def body(tokens, expert_ids, route_weights, gate_weight, up_weight, down_weight):
    devices_wide = lax.axis_size("expert")
    groups = lax.axis_size("tensor")
    experts = devices_wide // 2
    tok_count, per_token = expert_ids.shape
    width = tokens.shape[1]
    units = gate_weight.shape[1]
    capacity = min(tok_count, tok_count * per_token // experts)
    arrived_count = devices_wide * capacity

    packed = pl.pallas_call(
        lambda *refs: pack_kernel(capacity, 2, *refs),
        out_shape=jax.ShapeDtypeStruct((arrived_count, width), BF16),
        compiler_params=pltpu.CompilerParams(vmem_limit_bytes=VMEM_BYTES),
        name="pack",
    )(expert_ids, tokens)
    mix = pl.pallas_call(
        lambda *refs: mix_kernel(capacity, 2, *refs),
        out_shape=jax.ShapeDtypeStruct((tok_count, arrived_count), F32),
        compiler_params=pltpu.CompilerParams(vmem_limit_bytes=VMEM_BYTES),
        name="mix",
    )(expert_ids, route_weights)

    blocks = chip_blocks(gate_weight[0], up_weight[0], width, groups)
    arrived = lax.all_to_all(
        packed.reshape(devices_wide, capacity, width), "expert", 0, 0, tiled=True
    )
    arrived = arrived.reshape(arrived_count, width)
    down_near, down_far = down_columns(down_weight[0], width, groups)

    partner = lax.ppermute(arrived, "tensor", shift_pairs(groups, 0, 1))
    rings = groups // CORES
    near = pl.pallas_call(
        near_kernel,
        out_shape=jax.ShapeDtypeStruct((rings, 2 * units, arrived_count), F32),
        compiler_params=pltpu.CompilerParams(vmem_limit_bytes=VMEM_BYTES),
        cost_estimate=pl.CostEstimate(flops=10**9, bytes_accessed=10**6, transcendentals=0),
        name="near",
    )(arrived, *blocks)
    partial = pl.pallas_call(
        far_kernel,
        out_shape=jax.ShapeDtypeStruct((rings, 2 * units, arrived_count), BF16),
        compiler_params=pltpu.CompilerParams(vmem_limit_bytes=VMEM_BYTES),
        name="far",
    )(partner, near, *blocks)
    same_core = [list(range(core, groups, CORES)) for core in range(CORES)]
    partial = lax.all_to_all(
        partial, "tensor", 0, 0, axis_index_groups=same_core, tiled=True
    )
    hidden = pl.pallas_call(
        hidden_kernel,
        out_shape=jax.ShapeDtypeStruct((groups, units, arrived_count), BF16),
        compiler_params=pltpu.CompilerParams(vmem_limit_bytes=VMEM_BYTES),
        name="hidden",
    )(partial)
    hidden, mix = lax.optimization_barrier((hidden, mix))
    hidden = lax.all_to_all(hidden, "tensor", 0, 0, tiled=True)
    half_out = pl.pallas_call(
        down_kernel,
        out_shape=jax.ShapeDtypeStruct((arrived_count, width), BF16),
        scratch_shapes=[pltpu.VMEM((2, groups // 2 * units, arrived_count), BF16)],
        compiler_params=pltpu.CompilerParams(vmem_limit_bytes=VMEM_BYTES),
        name="down",
    )(hidden, down_near, down_far)
    returned = lax.all_to_all(
        half_out.reshape(devices_wide, capacity, width), "expert", 0, 0, tiled=True
    ).reshape(arrived_count, width)
    return pl.pallas_call(
        combine_kernel,
        out_shape=jax.ShapeDtypeStruct((tok_count, width), BF16),
        compiler_params=pltpu.CompilerParams(vmem_limit_bytes=VMEM_BYTES),
        name="combine",
    )(mix, returned)


def solution(mesh):
    placed = (
        P("expert", "tensor"),
        P("expert", None),
        P("expert", None),
        P("expert", "tensor", None),
        P("expert", "tensor", None),
        P("expert", "tensor", None),
    )
    def step(*args):
        return body(*args)

    step = jax.shard_map(
        step, mesh=mesh, in_specs=placed, out_specs=P("expert", "tensor"), check_vma=False
    )
    return step
```

```python
import jax
import jax.numpy as jnp
from jax import lax
from jax.experimental import pallas as pl
from jax.experimental.pallas import tpu as pltpu
from jax.sharding import PartitionSpec as P

F32 = jnp.float32
BF16 = jnp.bfloat16


def slot_onehot(ids, slots, capacity, copies):
    per_token, tok_count = ids.shape
    slot = lax.broadcasted_iota(jnp.int32, (slots, tok_count), 0)
    expert = slot // (capacity * copies)
    hit = jnp.zeros((slots, tok_count), F32)
    for j in range(per_token):
        hit = hit + jnp.where(ids[j : j + 1, :] == expert, 1.0, 0.0)
    row = lax.broadcasted_iota(jnp.int32, (tok_count, tok_count), 0)
    col = lax.broadcasted_iota(jnp.int32, (tok_count, tok_count), 1)
    before = jnp.where(row < col, 1.0, 0.0).astype(BF16)
    earlier = jnp.dot(hit.astype(BF16), before, preferred_element_type=F32)
    rank = (slot % capacity).astype(F32)
    return jnp.where((hit > 0.5) & (earlier == rank), 1.0, 0.0), expert


def pack_kernel(copies, ids_ref, tok_ref, out_ref):
    peers, capacity, width = out_ref.shape
    select, _ = slot_onehot(ids_ref[...], peers * capacity, capacity, copies)
    packed = jnp.dot(select.astype(BF16), tok_ref[...], preferred_element_type=F32)
    out_ref[...] = packed.reshape(peers, capacity, width).astype(BF16)


def mix_kernel(capacity, copies, ids_ref, route_ref, mix_ref):
    ids = ids_ref[...]
    route = route_ref[...]
    select, expert = slot_onehot(ids, mix_ref.shape[0], capacity, copies)
    weight = jnp.zeros(select.shape, F32)
    for j in range(ids.shape[0]):
        weight = weight + jnp.where(ids[j : j + 1, :] == expert, route[j : j + 1, :], 0.0)
    mix_ref[...] = select * weight


def combine_kernel(mix_ref, rows_ref, out_ref):
    mix = mix_ref[...]
    high = mix.astype(BF16)
    low = (mix - high.astype(F32)).astype(BF16)
    rows = rows_ref[...]
    dims = (((0,), (0,)), ((), ()))
    total = lax.dot_general(high, rows, dims, preferred_element_type=F32)
    total = total + lax.dot_general(low, rows, dims, preferred_element_type=F32)
    out_ref[...] = total.astype(BF16)


CORES = 2
VMEM_BYTES = 10 * 2**20


def moved_by(index, groups, ring, core, sign=1):
    rings = groups // CORES
    place = lax.rem(index // CORES + sign * ring + rings, rings)
    return place * CORES + lax.rem(lax.rem(index, CORES) + core, CORES)


def shift_pairs(groups, ring, core):
    rings = groups // CORES
    return [
        (i, (i // CORES + ring) % rings * CORES + (i + core) % CORES) for i in range(groups)
    ]


def cut_kernel(wide, gate_ref, up_ref, *outs):
    rings = len(outs)
    units = gate_ref.shape[0]
    chip = lax.axis_index("tensor") // CORES
    for ring, out in enumerate(outs):
        target = lax.rem(chip + ring, rings)
        cols = pl.ds(pl.multiple_of(target * wide, 128), wide)
        out[:units, :] = gate_ref[:, cols]
        out[units:, :] = up_ref[:, cols]


def chip_blocks(gate, up, width, groups):
    wide, rings = CORES * width, groups // CORES
    shape = jax.ShapeDtypeStruct((2 * gate.shape[0], wide), BF16)
    first, *rest = pl.pallas_call(
        lambda *refs: cut_kernel(wide, *refs),
        out_shape=[shape] * rings,
        name="cut",
    )(gate, up)
    return [first] + [
        lax.ppermute(block, "tensor", shift_pairs(groups, ring + 1, 0))
        for ring, block in enumerate(rest)
    ]


def half_product(block_ref, rows_ref, half):
    width = rows_ref.shape[1]
    cols = pl.ds(pl.multiple_of(half * width, 128), width)
    return lax.dot_general(
        block_ref[:, cols], rows_ref[...], (((1,), (1,)), ((), ())), preferred_element_type=F32
    )


def near_kernel(rows_ref, *refs):
    *blocks, out_ref = refs
    chip, core = lax.axis_index("tensor") // CORES, lax.rem(lax.axis_index("tensor"), CORES)
    for ring, block in enumerate(blocks):
        source = lax.rem(chip - ring + len(blocks), len(blocks))
        out_ref[source] = half_product(block, rows_ref, core)


def far_kernel(rows_ref, near_ref, *refs):
    *blocks, out_ref = refs
    chip, core = lax.axis_index("tensor") // CORES, lax.rem(lax.axis_index("tensor"), CORES)
    for ring, block in enumerate(blocks):
        source = lax.rem(chip - ring + len(blocks), len(blocks))
        out_ref[source] = (near_ref[source] + half_product(block, rows_ref, 1 - core)).astype(BF16)


def hidden_kernel(partial_ref, out_ref):
    groups, units, _ = out_ref.shape
    act = partial_ref[0].astype(F32)
    for g in range(1, partial_ref.shape[0]):
        act = act + partial_ref[g].astype(F32)
    gate, up = act[:units], act[units:]
    hidden = (jax.nn.silu(gate) * up).astype(BF16)
    for g in range(groups):
        out_ref[g] = hidden


def chip_cut_kernel(wide, weight_ref, *outs):
    rings = len(outs)
    chip = lax.axis_index("tensor") // CORES
    for ring, out in enumerate(outs):
        target = lax.rem(chip + ring, rings)
        out[...] = weight_ref[:, pl.ds(pl.multiple_of(target * wide, 128), wide)]


def core_cut_kernel(*refs):
    *blocks, near_ref, far_ref = refs
    core = lax.rem(lax.axis_index("tensor"), CORES)
    units = blocks[0].shape[0]
    width = near_ref.shape[1]
    for ring, block in enumerate(blocks):
        rows = pl.ds(ring * units, units)
        near_ref[rows, :] = block[:, pl.ds(pl.multiple_of(core * width, 128), width)]
        far_ref[rows, :] = block[:, pl.ds(pl.multiple_of((1 - core) * width, 128), width)]


def down_columns(weight, width, groups):
    units = weight.shape[0]
    rings, wide = groups // CORES, CORES * width
    first, *rest = pl.pallas_call(
        lambda *refs: chip_cut_kernel(wide, *refs),
        out_shape=[jax.ShapeDtypeStruct((units, wide), BF16)] * rings,
        name="chip_cut",
    )(weight)
    for ring in range(1, rings):
        rest[ring - 1] = lax.ppermute(
            rest[ring - 1], "tensor", shift_pairs(groups, ring, 0)
        )
    near, far = pl.pallas_call(
        core_cut_kernel,
        out_shape=[jax.ShapeDtypeStruct((rings * units, width), BF16)] * 2,
        compiler_params=pltpu.CompilerParams(vmem_limit_bytes=VMEM_BYTES),
        name="core_cut",
    )(first, *rest)
    return near, lax.ppermute(far, "tensor", shift_pairs(groups, 0, 1))


def down_kernel(hidden_ref, near_ref, far_ref, out_ref, held):
    groups, units, _ = hidden_ref.shape
    me = lax.axis_index("tensor")
    for core in range(CORES):
        for ring in range(groups // CORES):
            source = moved_by(me, groups, ring, core, sign=-1)
            held[core, pl.ds(ring * units, units), :] = hidden_ref[source]
    dims = (((0,), (0,)), ((), ()))
    total = lax.dot_general(held[0], near_ref[...], dims, preferred_element_type=F32)
    total = total + lax.dot_general(held[1], far_ref[...], dims, preferred_element_type=F32)
    out_ref[...] = total.astype(BF16)


def body(tokens, expert_ids, route_weights, gate_weight, up_weight, down_weight):
    devices_wide = lax.axis_size("expert")
    groups = lax.axis_size("tensor")
    experts = devices_wide // 2
    tok_count, per_token = expert_ids.shape
    width = tokens.shape[1]
    units = gate_weight.shape[1]
    capacity = min(tok_count, tok_count * per_token // experts)
    arrived_count = devices_wide * capacity

    ids = expert_ids.T
    packed = pl.pallas_call(
        lambda *refs: pack_kernel(2, *refs),
        out_shape=jax.ShapeDtypeStruct((devices_wide, capacity, width), BF16),
        name="pack",
    )(ids, tokens)
    mix = pl.pallas_call(
        lambda *refs: mix_kernel(capacity, 2, *refs),
        out_shape=jax.ShapeDtypeStruct((arrived_count, tok_count), F32),
        compiler_params=pltpu.CompilerParams(vmem_limit_bytes=VMEM_BYTES),
        name="mix",
    )(ids, route_weights.T)

    blocks = chip_blocks(gate_weight[0], up_weight[0], width, groups)
    arrived = lax.all_to_all(packed, "expert", 0, 0, tiled=True)
    arrived = arrived.reshape(arrived_count, width)
    down_near, down_far = down_columns(down_weight[0], width, groups)

    partner = lax.ppermute(arrived, "tensor", shift_pairs(groups, 0, 1))
    rings = groups // CORES
    near = pl.pallas_call(
        near_kernel,
        out_shape=jax.ShapeDtypeStruct((rings, 2 * units, arrived_count), F32),
        compiler_params=pltpu.CompilerParams(vmem_limit_bytes=VMEM_BYTES),
        cost_estimate=pl.CostEstimate(flops=10**9, bytes_accessed=10**6, transcendentals=0),
        name="near",
    )(arrived, *blocks)
    partial = pl.pallas_call(
        far_kernel,
        out_shape=jax.ShapeDtypeStruct((rings, 2 * units, arrived_count), BF16),
        compiler_params=pltpu.CompilerParams(vmem_limit_bytes=VMEM_BYTES),
        name="far",
    )(partner, near, *blocks)
    same_core = [list(range(core, groups, CORES)) for core in range(CORES)]
    partial = lax.all_to_all(
        partial, "tensor", 0, 0, axis_index_groups=same_core, tiled=True
    )
    hidden = pl.pallas_call(
        hidden_kernel,
        out_shape=jax.ShapeDtypeStruct((groups, units, arrived_count), BF16),
        compiler_params=pltpu.CompilerParams(vmem_limit_bytes=VMEM_BYTES),
        name="hidden",
    )(partial)
    hidden, mix = lax.optimization_barrier((hidden, mix))
    hidden = lax.all_to_all(hidden, "tensor", 0, 0, tiled=True)
    half_out = pl.pallas_call(
        down_kernel,
        out_shape=jax.ShapeDtypeStruct((arrived_count, width), BF16),
        scratch_shapes=[pltpu.VMEM((2, groups // 2 * units, arrived_count), BF16)],
        compiler_params=pltpu.CompilerParams(vmem_limit_bytes=VMEM_BYTES),
        name="down",
    )(hidden, down_near, down_far)
    returned = lax.all_to_all(
        half_out.reshape(devices_wide, capacity, width), "expert", 0, 0, tiled=True
    ).reshape(arrived_count, width)
    return pl.pallas_call(
        combine_kernel,
        out_shape=jax.ShapeDtypeStruct((tok_count, width), BF16),
        compiler_params=pltpu.CompilerParams(vmem_limit_bytes=VMEM_BYTES),
        name="combine",
    )(mix, returned)


def solution(mesh):
    placed = (
        P("expert", "tensor"),
        P("expert", None),
        P("expert", None),
        P("expert", "tensor", None),
        P("expert", "tensor", None),
        P("expert", "tensor", None),
    )
    def step(*args):
        return body(*args)

    step = jax.shard_map(
        step, mesh=mesh, in_specs=placed, out_specs=P("expert", "tensor"), check_vma=False
    )
    return step
```

```python
import jax
import jax.numpy as jnp
from jax import lax
from jax.experimental import pallas as pl
from jax.experimental.pallas import tpu as pltpu
from jax.sharding import PartitionSpec as P

F32 = jnp.float32
BF16 = jnp.bfloat16


def slot_onehot(ids, slots, capacity, copies):
    per_token, tok_count = ids.shape
    slot = lax.broadcasted_iota(jnp.int32, (slots, tok_count), 0)
    expert = slot // (capacity * copies)
    hit = jnp.zeros((slots, tok_count), F32)
    for j in range(per_token):
        hit = hit + jnp.where(ids[j : j + 1, :] == expert, 1.0, 0.0)
    row = lax.broadcasted_iota(jnp.int32, (tok_count, tok_count), 0)
    col = lax.broadcasted_iota(jnp.int32, (tok_count, tok_count), 1)
    before = jnp.where(row < col, 1.0, 0.0).astype(BF16)
    earlier = jnp.dot(hit.astype(BF16), before, preferred_element_type=F32)
    rank = (slot % capacity).astype(F32)
    return jnp.where((hit > 0.5) & (earlier == rank), 1.0, 0.0), expert


def pack_kernel(copies, ids_ref, tok_ref, out_ref):
    peers, capacity, width = out_ref.shape
    select, _ = slot_onehot(ids_ref[...], peers * capacity, capacity, copies)
    packed = jnp.dot(select.astype(BF16), tok_ref[...], preferred_element_type=F32)
    out_ref[...] = packed.reshape(peers, capacity, width).astype(BF16)


def mix_kernel(capacity, copies, ids_ref, route_ref, mix_ref):
    ids = ids_ref[...]
    route = route_ref[...]
    select, expert = slot_onehot(ids, mix_ref.shape[0], capacity, copies)
    weight = jnp.zeros(select.shape, F32)
    for j in range(ids.shape[0]):
        weight = weight + jnp.where(ids[j : j + 1, :] == expert, route[j : j + 1, :], 0.0)
    mix_ref[...] = select * weight


def combine_kernel(mix_ref, rows_ref, out_ref):
    mix = mix_ref[...]
    high = mix.astype(BF16)
    low = (mix - high.astype(F32)).astype(BF16)
    rows = rows_ref[...]
    dims = (((0,), (0,)), ((), ()))
    total = lax.dot_general(high, rows, dims, preferred_element_type=F32)
    total = total + lax.dot_general(low, rows, dims, preferred_element_type=F32)
    out_ref[...] = total.astype(BF16)


CORES = 2
VMEM_BYTES = 10 * 2**20


def moved_by(index, groups, ring, core, sign=1):
    rings = groups // CORES
    place = lax.rem(index // CORES + sign * ring + rings, rings)
    return place * CORES + lax.rem(lax.rem(index, CORES) + core, CORES)


def shift_pairs(groups, ring, core):
    rings = groups // CORES
    return [
        (i, (i // CORES + ring) % rings * CORES + (i + core) % CORES) for i in range(groups)
    ]


def cut_kernel(wide, gate_ref, up_ref, *refs):
    *outs, held, taken, given = refs
    rings = len(outs)
    units = gate_ref.shape[0]
    chip = lax.axis_index("tensor") // CORES
    order = [ring % rings for ring in range(1, rings + 1)]
    reads, writes = {}, {}
    for ring in order:
        cols = pl.ds(pl.multiple_of(lax.rem(chip + ring, rings) * wide, 128), wide)
        for part, weight in enumerate((gate_ref, up_ref)):
            reads[ring, part] = pltpu.make_async_copy(
                weight.at[:, cols],
                held.at[ring, pl.ds(part * units, units), :],
                taken.at[ring, part],
            )
            reads[ring, part].start()
    for ring in order:
        reads[ring, 0].wait()
        reads[ring, 1].wait()
        writes[ring] = pltpu.make_async_copy(held.at[ring], outs[ring], given.at[ring])
        writes[ring].start()
    for ring in order:
        writes[ring].wait()


def chip_blocks(gate, up, width, groups):
    wide, rings = CORES * width, groups // CORES
    shape = jax.ShapeDtypeStruct((2 * gate.shape[0], wide), BF16)
    whole = pl.BlockSpec(memory_space=pl.ANY)
    blocks = pl.pallas_call(
        lambda *refs: cut_kernel(wide, *refs),
        out_shape=[shape] * rings,
        in_specs=[whole] * 2,
        out_specs=[whole] * rings,
        scratch_shapes=[
            pltpu.VMEM((rings, *shape.shape), BF16),
            pltpu.SemaphoreType.DMA((rings, 2)),
            pltpu.SemaphoreType.DMA((rings,)),
        ],
        name="cut",
    )(gate, up)
    blocks = list(blocks)
    for ring in range(1, rings):
        blocks[ring] = lax.ppermute(
            blocks[ring], "tensor", shift_pairs(groups, ring, 0)
        )
    return blocks


def half_product(block_ref, rows_ref, half):
    width = rows_ref.shape[1]
    cols = pl.ds(pl.multiple_of(half * width, 128), width)
    return lax.dot_general(
        block_ref[:, cols], rows_ref[...], (((1,), (1,)), ((), ())), preferred_element_type=F32
    )


def near_kernel(rows_ref, *refs):
    *blocks, out_ref = refs
    chip, core = lax.axis_index("tensor") // CORES, lax.rem(lax.axis_index("tensor"), CORES)
    for ring, block in enumerate(blocks):
        source = lax.rem(chip - ring + len(blocks), len(blocks))
        out_ref[source] = half_product(block, rows_ref, core)


def far_kernel(rows_ref, near_ref, *refs):
    *blocks, out_ref = refs
    chip, core = lax.axis_index("tensor") // CORES, lax.rem(lax.axis_index("tensor"), CORES)
    for ring, block in enumerate(blocks):
        source = lax.rem(chip - ring + len(blocks), len(blocks))
        out_ref[source] = (near_ref[source] + half_product(block, rows_ref, 1 - core)).astype(BF16)


def hidden_kernel(partial_ref, out_ref):
    groups, units, _ = out_ref.shape
    act = partial_ref[0].astype(F32)
    for g in range(1, partial_ref.shape[0]):
        act = act + partial_ref[g].astype(F32)
    gate, up = act[:units], act[units:]
    hidden = (jax.nn.silu(gate) * up).astype(BF16)
    for g in range(groups):
        out_ref[g] = hidden


def split_kernel(weight_ref, keep_ref, send_ref, held, taken, given):
    rings, _, width = keep_ref.shape
    core = lax.rem(lax.axis_index("tensor"), CORES)
    reads = []
    for side in (1, 0):
        lane = lax.rem(core + side, CORES)
        for ring in range(rings):
            cols = pl.ds(pl.multiple_of((ring * CORES + lane) * width, 128), width)
            reads.append(
                pltpu.make_async_copy(
                    weight_ref.at[:, cols], held.at[side, ring], taken.at[side, ring]
                )
            )
            reads[-1].start()
    writes = []
    for place, (side, out) in enumerate(((1, send_ref), (0, keep_ref))):
        for read in reads[place * rings : (place + 1) * rings]:
            read.wait()
        writes.append(pltpu.make_async_copy(held.at[side], out, given.at[side]))
        writes[-1].start()
    for write in writes:
        write.wait()


def join_kernel(keep_ref, took_ref, *outs):
    rings, units, _ = keep_ref.shape
    chip = lax.axis_index("tensor") // CORES
    for ring, out in enumerate(outs):
        target = lax.rem(chip + ring, rings)
        out[:units, :] = keep_ref[target]
        out[units:, :] = took_ref[target]


def down_blocks(weight, width, groups):
    units = weight.shape[0]
    rings = groups // CORES
    whole = pl.BlockSpec(memory_space=pl.ANY)
    keep, send = pl.pallas_call(
        split_kernel,
        out_shape=[jax.ShapeDtypeStruct((rings, units, width), BF16)] * 2,
        in_specs=[whole],
        out_specs=[whole] * 2,
        scratch_shapes=[
            pltpu.VMEM((CORES, rings, units, width), BF16),
            pltpu.SemaphoreType.DMA((CORES, rings)),
            pltpu.SemaphoreType.DMA((CORES,)),
        ],
        name="split",
    )(weight)
    took = lax.ppermute(send, "tensor", shift_pairs(groups, 0, 1))
    blocks = pl.pallas_call(
        join_kernel,
        out_shape=[jax.ShapeDtypeStruct((CORES * units, width), BF16)] * rings,
        name="join",
    )(keep, took)
    blocks = list(blocks)
    for ring in range(1, rings):
        blocks[ring] = lax.ppermute(
            blocks[ring], "tensor", shift_pairs(groups, ring, 0)
        )
    return blocks


def down_kernel(hidden_ref, *refs):
    *blocks, out_ref, held = refs
    groups, units, _ = hidden_ref.shape
    me = lax.axis_index("tensor")
    total = None
    for ring, block in enumerate(blocks):
        for core in range(CORES):
            source = moved_by(me, groups, ring, core, sign=-1)
            held[ring, pl.ds(core * units, units), :] = hidden_ref[source]
        term = lax.dot_general(
            held[ring], block[...], (((0,), (0,)), ((), ())), preferred_element_type=F32
        )
        total = term if total is None else total + term
    out_ref[...] = total.astype(BF16)


def body(tokens, expert_ids, route_weights, gate_weight, up_weight, down_weight):
    devices_wide = lax.axis_size("expert")
    groups = lax.axis_size("tensor")
    experts = devices_wide // 2
    tok_count, per_token = expert_ids.shape
    width = tokens.shape[1]
    units = gate_weight.shape[1]
    capacity = min(tok_count, tok_count * per_token // experts)
    arrived_count = devices_wide * capacity

    ids = expert_ids.T
    packed = pl.pallas_call(
        lambda *refs: pack_kernel(2, *refs),
        out_shape=jax.ShapeDtypeStruct((devices_wide, capacity, width), BF16),
        name="pack",
    )(ids, tokens)
    mix = pl.pallas_call(
        lambda *refs: mix_kernel(capacity, 2, *refs),
        out_shape=jax.ShapeDtypeStruct((arrived_count, tok_count), F32),
        compiler_params=pltpu.CompilerParams(vmem_limit_bytes=VMEM_BYTES),
        name="mix",
    )(ids, route_weights.T)

    blocks = chip_blocks(gate_weight[0], up_weight[0], width, groups)
    arrived = lax.all_to_all(packed, "expert", 0, 0, tiled=True)
    arrived = arrived.reshape(arrived_count, width)
    down = down_blocks(down_weight[0], width, groups)

    partner = lax.ppermute(arrived, "tensor", shift_pairs(groups, 0, 1))
    rings = groups // CORES
    near = pl.pallas_call(
        near_kernel,
        out_shape=jax.ShapeDtypeStruct((rings, 2 * units, arrived_count), F32),
        compiler_params=pltpu.CompilerParams(vmem_limit_bytes=VMEM_BYTES),
        cost_estimate=pl.CostEstimate(flops=10**9, bytes_accessed=10**6, transcendentals=0),
        name="near",
    )(arrived, *blocks)
    partial = pl.pallas_call(
        far_kernel,
        out_shape=jax.ShapeDtypeStruct((rings, 2 * units, arrived_count), BF16),
        compiler_params=pltpu.CompilerParams(vmem_limit_bytes=VMEM_BYTES),
        name="far",
    )(partner, near, *blocks)
    same_core = [list(range(core, groups, CORES)) for core in range(CORES)]
    partial = lax.all_to_all(
        partial, "tensor", 0, 0, axis_index_groups=same_core, tiled=True
    )
    hidden = pl.pallas_call(
        hidden_kernel,
        out_shape=jax.ShapeDtypeStruct((groups, units, arrived_count), BF16),
        compiler_params=pltpu.CompilerParams(vmem_limit_bytes=VMEM_BYTES),
        name="hidden",
    )(partial)
    hidden, mix = lax.optimization_barrier((hidden, mix))
    hidden = lax.all_to_all(hidden, "tensor", 0, 0, tiled=True)
    half_out = pl.pallas_call(
        down_kernel,
        out_shape=jax.ShapeDtypeStruct((arrived_count, width), BF16),
        scratch_shapes=[pltpu.VMEM((rings, CORES * units, arrived_count), BF16)],
        compiler_params=pltpu.CompilerParams(vmem_limit_bytes=VMEM_BYTES),
        name="down",
    )(hidden, *down)
    returned = lax.all_to_all(
        half_out.reshape(devices_wide, capacity, width), "expert", 0, 0, tiled=True
    ).reshape(arrived_count, width)
    return pl.pallas_call(
        combine_kernel,
        out_shape=jax.ShapeDtypeStruct((tok_count, width), BF16),
        compiler_params=pltpu.CompilerParams(vmem_limit_bytes=VMEM_BYTES),
        name="combine",
    )(mix, returned)


def solution(mesh):
    placed = (
        P("expert", "tensor"),
        P("expert", None),
        P("expert", None),
        P("expert", "tensor", None),
        P("expert", "tensor", None),
        P("expert", "tensor", None),
    )
    def step(*args):
        return body(*args)

    step = jax.shard_map(
        step, mesh=mesh, in_specs=placed, out_specs=P("expert", "tensor"), check_vma=False
    )
    return step
```

```python
import jax
import jax.numpy as jnp
from jax import lax
from jax.experimental import pallas as pl
from jax.experimental.pallas import tpu as pltpu
from jax.sharding import PartitionSpec as P

F32 = jnp.float32
BF16 = jnp.bfloat16


def slot_onehot(ids, slots, capacity, copies):
    per_token, tok_count = ids.shape
    slot = lax.broadcasted_iota(jnp.int32, (slots, tok_count), 0)
    expert = slot // (capacity * copies)
    hit = jnp.zeros((slots, tok_count), F32)
    for j in range(per_token):
        hit = hit + jnp.where(ids[j : j + 1, :] == expert, 1.0, 0.0)
    row = lax.broadcasted_iota(jnp.int32, (tok_count, tok_count), 0)
    col = lax.broadcasted_iota(jnp.int32, (tok_count, tok_count), 1)
    before = jnp.where(row < col, 1.0, 0.0).astype(BF16)
    earlier = jnp.dot(hit.astype(BF16), before, preferred_element_type=F32)
    rank = (slot % capacity).astype(F32)
    return jnp.where((hit > 0.5) & (earlier == rank), 1.0, 0.0), expert


def pack_kernel(copies, ring, ids_ref, tok_ref, gate_ref, up_ref, out_ref, block_ref, *refs):
    held, taken, given = refs
    reads = cut_reads(ring, (gate_ref, up_ref), held, taken)
    peers, capacity, width = out_ref.shape
    select, _ = slot_onehot(ids_ref[...], peers * capacity, capacity, copies)
    packed = jnp.dot(select.astype(BF16), tok_ref[...], preferred_element_type=F32)
    for read in reads:
        read.wait()
    write = pltpu.make_async_copy(held, block_ref, given)
    write.start()
    out_ref[...] = packed.reshape(peers, capacity, width).astype(BF16)
    write.wait()


def mix_kernel(capacity, copies, ids_ref, route_ref, mix_ref):
    ids = ids_ref[...]
    route = route_ref[...]
    select, expert = slot_onehot(ids, mix_ref.shape[0], capacity, copies)
    weight = jnp.zeros(select.shape, F32)
    for j in range(ids.shape[0]):
        weight = weight + jnp.where(ids[j : j + 1, :] == expert, route[j : j + 1, :], 0.0)
    mix_ref[...] = select * weight


def combine_kernel(mix_ref, rows_ref, out_ref):
    mix = mix_ref[...]
    high = mix.astype(BF16)
    low = (mix - high.astype(F32)).astype(BF16)
    rows = rows_ref[...]
    dims = (((0,), (0,)), ((), ()))
    total = lax.dot_general(high, rows, dims, preferred_element_type=F32)
    total = total + lax.dot_general(low, rows, dims, preferred_element_type=F32)
    out_ref[...] = total.astype(BF16)


CORES = 2
VMEM_BYTES = 10 * 2**20


def moved_by(index, groups, ring, core, sign=1):
    rings = groups // CORES
    place = lax.rem(index // CORES + sign * ring + rings, rings)
    return place * CORES + lax.rem(lax.rem(index, CORES) + core, CORES)


def shift_pairs(groups, ring, core):
    rings = groups // CORES
    return [
        (i, (i // CORES + ring) % rings * CORES + (i + core) % CORES) for i in range(groups)
    ]


def cut_reads(ring, weights, held, taken):
    wide = held.shape[1]
    units, full = weights[0].shape
    rings = full // wide
    chip = lax.axis_index("tensor") // CORES
    cols = pl.ds(pl.multiple_of(lax.rem(chip + ring, rings) * wide, 128), wide)
    reads = []
    for part, weight in enumerate(weights):
        reads.append(
            pltpu.make_async_copy(
                weight.at[:, cols], held.at[pl.ds(part * units, units), :], taken.at[part]
            )
        )
        reads[-1].start()
    return reads


def cut_kernel(rings, parts, *refs):
    weights, refs = refs[:parts], refs[parts:]
    *outs, held, taken, given = refs
    reads = [
        cut_reads(ring, weights, held.at[place], taken.at[place])
        for place, ring in enumerate(rings)
    ]
    writes = []
    for place, out in enumerate(outs):
        for read in reads[place]:
            read.wait()
        writes.append(pltpu.make_async_copy(held.at[place], out, given.at[place]))
        writes[-1].start()
    for write in writes:
        write.wait()


def cut(rings, weights, wide):
    parts, units = len(weights), weights[0].shape[0]
    shape = jax.ShapeDtypeStruct((parts * units, wide), BF16)
    whole = pl.BlockSpec(memory_space=pl.ANY)
    return pl.pallas_call(
        lambda *refs: cut_kernel(rings, parts, *refs),
        out_shape=[shape] * len(rings),
        in_specs=[whole] * parts,
        out_specs=[whole] * len(rings),
        scratch_shapes=[
            pltpu.VMEM((len(rings), *shape.shape), BF16),
            pltpu.SemaphoreType.DMA((len(rings), parts)),
            pltpu.SemaphoreType.DMA((len(rings),)),
        ],
        name="cut",
    )(*weights)


def half_product(block_ref, rows_ref, half):
    width = rows_ref.shape[1]
    cols = pl.ds(pl.multiple_of(half * width, 128), width)
    return lax.dot_general(
        block_ref[:, cols], rows_ref[...], (((1,), (1,)), ((), ())), preferred_element_type=F32
    )


def near_kernel(rows_ref, *refs):
    *blocks, out_ref = refs
    chip, core = lax.axis_index("tensor") // CORES, lax.rem(lax.axis_index("tensor"), CORES)
    for ring, block in enumerate(blocks):
        source = lax.rem(chip - ring + len(blocks), len(blocks))
        out_ref[source] = half_product(block, rows_ref, core)


def far_kernel(rows_ref, near_ref, *refs):
    *blocks, out_ref = refs
    chip, core = lax.axis_index("tensor") // CORES, lax.rem(lax.axis_index("tensor"), CORES)
    for ring, block in enumerate(blocks):
        source = lax.rem(chip - ring + len(blocks), len(blocks))
        out_ref[source] = (near_ref[source] + half_product(block, rows_ref, 1 - core)).astype(BF16)


def hidden_kernel(partial_ref, out_ref):
    groups, units, _ = out_ref.shape
    act = partial_ref[0].astype(F32)
    for g in range(1, partial_ref.shape[0]):
        act = act + partial_ref[g].astype(F32)
    gate, up = act[:units], act[units:]
    hidden = (jax.nn.silu(gate) * up).astype(BF16)
    for g in range(groups):
        out_ref[g] = hidden


def core_cut_kernel(*refs):
    *blocks, near_ref, far_ref = refs
    core = lax.rem(lax.axis_index("tensor"), CORES)
    units = blocks[0].shape[0]
    width = near_ref.shape[1]
    for ring, block in enumerate(blocks):
        rows = pl.ds(ring * units, units)
        near_ref[rows, :] = block[:, pl.ds(pl.multiple_of(core * width, 128), width)]
        far_ref[rows, :] = block[:, pl.ds(pl.multiple_of((1 - core) * width, 128), width)]


def down_columns(weight, width, groups):
    units = weight.shape[0]
    rings = groups // CORES
    order = (1, 2, 3, 0)
    cuts = cut(order, (weight,), CORES * width)
    blocks = dict(zip(order, cuts))
    for ring in range(1, rings):
        blocks[ring] = lax.ppermute(
            blocks[ring], "tensor", shift_pairs(groups, ring, 0)
        )
    near, far = pl.pallas_call(
        core_cut_kernel,
        out_shape=[jax.ShapeDtypeStruct((rings * units, width), BF16)] * 2,
        compiler_params=pltpu.CompilerParams(vmem_limit_bytes=VMEM_BYTES),
        name="core_cut",
    )(*[blocks[ring] for ring in range(rings)])
    return near, lax.ppermute(far, "tensor", shift_pairs(groups, 0, 1))


def down_kernel(hidden_ref, near_ref, far_ref, out_ref, held):
    groups, units, _ = hidden_ref.shape
    me = lax.axis_index("tensor")
    for core in range(CORES):
        for ring in range(groups // CORES):
            source = moved_by(me, groups, ring, core, sign=-1)
            held[core, pl.ds(ring * units, units), :] = hidden_ref[source]
    dims = (((0,), (0,)), ((), ()))
    total = lax.dot_general(held[0], near_ref[...], dims, preferred_element_type=F32)
    total = total + lax.dot_general(held[1], far_ref[...], dims, preferred_element_type=F32)
    out_ref[...] = total.astype(BF16)


def body(tokens, expert_ids, route_weights, gate_weight, up_weight, down_weight):
    devices_wide = lax.axis_size("expert")
    groups = lax.axis_size("tensor")
    experts = devices_wide // 2
    tok_count, per_token = expert_ids.shape
    width = tokens.shape[1]
    units = gate_weight.shape[1]
    capacity = min(tok_count, tok_count * per_token // experts)
    arrived_count = devices_wide * capacity

    ids = expert_ids.T
    rings, wide = groups // CORES, CORES * width
    gate_up = (gate_weight[0], up_weight[0])
    part = jax.ShapeDtypeStruct((2 * units, wide), BF16)
    whole, held = pl.BlockSpec(memory_space=pl.ANY), pl.BlockSpec(memory_space=pltpu.VMEM)
    packed, across = pl.pallas_call(
        lambda *refs: pack_kernel(2, 2, *refs),
        out_shape=[jax.ShapeDtypeStruct((devices_wide, capacity, width), BF16), part],
        in_specs=[held, held, whole, whole],
        out_specs=[held, whole],
        scratch_shapes=[
            pltpu.VMEM(part.shape, BF16),
            pltpu.SemaphoreType.DMA((2,)),
            pltpu.SemaphoreType.DMA,
        ],
        name="pack",
    )(ids, tokens, *gate_up)
    mix = pl.pallas_call(
        lambda *refs: mix_kernel(capacity, 2, *refs),
        out_shape=jax.ShapeDtypeStruct((arrived_count, tok_count), F32),
        compiler_params=pltpu.CompilerParams(vmem_limit_bytes=VMEM_BYTES),
        name="mix",
    )(ids, route_weights.T)

    ahead, behind, own = cut((1, 3, 0), gate_up, wide)
    blocks = [own, ahead, across, behind]
    for ring in range(1, rings):
        blocks[ring] = lax.ppermute(
            blocks[ring], "tensor", shift_pairs(groups, ring, 0)
        )
    arrived = lax.all_to_all(packed, "expert", 0, 0, tiled=True)
    arrived = arrived.reshape(arrived_count, width)
    down_near, down_far = down_columns(down_weight[0], width, groups)

    partner = lax.ppermute(arrived, "tensor", shift_pairs(groups, 0, 1))
    near = pl.pallas_call(
        near_kernel,
        out_shape=jax.ShapeDtypeStruct((rings, 2 * units, arrived_count), F32),
        compiler_params=pltpu.CompilerParams(vmem_limit_bytes=VMEM_BYTES),
        cost_estimate=pl.CostEstimate(flops=10**9, bytes_accessed=10**6, transcendentals=0),
        name="near",
    )(arrived, *blocks)
    partial = pl.pallas_call(
        far_kernel,
        out_shape=jax.ShapeDtypeStruct((rings, 2 * units, arrived_count), BF16),
        compiler_params=pltpu.CompilerParams(vmem_limit_bytes=VMEM_BYTES),
        name="far",
    )(partner, near, *blocks)
    same_core = [list(range(core, groups, CORES)) for core in range(CORES)]
    partial = lax.all_to_all(
        partial, "tensor", 0, 0, axis_index_groups=same_core, tiled=True
    )
    hidden = pl.pallas_call(
        hidden_kernel,
        out_shape=jax.ShapeDtypeStruct((groups, units, arrived_count), BF16),
        compiler_params=pltpu.CompilerParams(vmem_limit_bytes=VMEM_BYTES),
        name="hidden",
    )(partial)
    hidden, mix = lax.optimization_barrier((hidden, mix))
    hidden = lax.all_to_all(hidden, "tensor", 0, 0, tiled=True)
    half_out = pl.pallas_call(
        down_kernel,
        out_shape=jax.ShapeDtypeStruct((arrived_count, width), BF16),
        scratch_shapes=[pltpu.VMEM((2, groups // 2 * units, arrived_count), BF16)],
        compiler_params=pltpu.CompilerParams(vmem_limit_bytes=VMEM_BYTES),
        name="down",
    )(hidden, down_near, down_far)
    returned = lax.all_to_all(
        half_out.reshape(devices_wide, capacity, width), "expert", 0, 0, tiled=True
    ).reshape(arrived_count, width)
    return pl.pallas_call(
        combine_kernel,
        out_shape=jax.ShapeDtypeStruct((tok_count, width), BF16),
        compiler_params=pltpu.CompilerParams(vmem_limit_bytes=VMEM_BYTES),
        name="combine",
    )(mix, returned)


def solution(mesh):
    placed = (
        P("expert", "tensor"),
        P("expert", None),
        P("expert", None),
        P("expert", "tensor", None),
        P("expert", "tensor", None),
        P("expert", "tensor", None),
    )
    def step(*args):
        return body(*args)

    step = jax.shard_map(
        step, mesh=mesh, in_specs=placed, out_specs=P("expert", "tensor"), check_vma=False
    )
    return step
```

```python
import jax
import jax.numpy as jnp
from jax import lax
from jax.experimental import pallas as pl
from jax.experimental.pallas import tpu as pltpu
from jax.sharding import Mesh, PartitionSpec as P

F32 = jnp.float32
BF16 = jnp.bfloat16


def slot_onehot(ids, slots, capacity, copies):
    per_token, tok_count = ids.shape
    slot = lax.broadcasted_iota(jnp.int32, (slots, tok_count), 0)
    expert = slot // (capacity * copies)
    hit = jnp.zeros((slots, tok_count), F32)
    for j in range(per_token):
        hit = hit + jnp.where(ids[j : j + 1, :] == expert, 1.0, 0.0)
    row = lax.broadcasted_iota(jnp.int32, (tok_count, tok_count), 0)
    col = lax.broadcasted_iota(jnp.int32, (tok_count, tok_count), 1)
    before = jnp.where(row < col, 1.0, 0.0).astype(BF16)
    earlier = jnp.dot(hit.astype(BF16), before, preferred_element_type=F32)
    rank = (slot % capacity).astype(F32)
    return jnp.where((hit > 0.5) & (earlier == rank), 1.0, 0.0), expert


def pack_kernel(copies, ring, ids_ref, tok_ref, gate_ref, up_ref, out_ref, block_ref, *refs):
    held, taken, given = refs
    reads = cut_reads(ring, (gate_ref, up_ref), held, taken)
    peers, capacity, width = out_ref.shape
    select, _ = slot_onehot(ids_ref[...], peers * capacity, capacity, copies)
    packed = jnp.dot(select.astype(BF16), tok_ref[...], preferred_element_type=F32)
    for read in reads:
        read.wait()
    write = pltpu.make_async_copy(held, block_ref, given)
    write.start()
    out_ref[...] = packed.reshape(peers, capacity, width).astype(BF16)
    write.wait()


def mix_kernel(capacity, copies, ids_ref, route_ref, mix_ref):
    ids = ids_ref[...]
    route = route_ref[...]
    select, expert = slot_onehot(ids, mix_ref.shape[0], capacity, copies)
    weight = jnp.zeros(select.shape, F32)
    for j in range(ids.shape[0]):
        weight = weight + jnp.where(ids[j : j + 1, :] == expert, route[j : j + 1, :], 0.0)
    mix_ref[...] = select * weight


def combine_kernel(capacity, mix_ref, rows_ref, out_ref):
    half = rows_ref.shape[1]
    width = out_ref.shape[1]
    row = lax.broadcasted_iota(jnp.int32, mix_ref.shape, 0)
    first = lax.rem(row // capacity, 2) == 0
    for place in range(2):
        mix = jnp.where(first == (place == 0), mix_ref[...], 0.0)
        high = mix.astype(BF16)
        low = (mix - high.astype(F32)).astype(BF16)
        rows = rows_ref[...] if place == 0 else rows_ref[:, 2 * half - width :]
        dims = (((0,), (0,)), ((), ()))
        total = lax.dot_general(high, rows, dims, preferred_element_type=F32)
        total = total + lax.dot_general(low, rows, dims, preferred_element_type=F32)
        cols = slice(0, half) if place == 0 else slice(half, width)
        out_ref[:, cols] = total.astype(BF16)


CORES = 2
EXPERT = ("pair", "half")
QUARTERS = [(0, 0), (0, 1), (1, 0), (1, 1)]
VMEM_BYTES = 10 * 2**20


def moved_by(index, groups, ring, core, sign=1):
    rings = groups // CORES
    place = lax.rem(index // CORES + sign * ring + rings, rings)
    return place * CORES + lax.rem(lax.rem(index, CORES) + core, CORES)


def shift_pairs(groups, ring, core):
    rings = groups // CORES
    return [
        (i, (i // CORES + ring) % rings * CORES + (i + core) % CORES) for i in range(groups)
    ]


def cut_reads(ring, weights, held, taken):
    wide = held.shape[1]
    units, full = weights[0].shape
    rings = full // wide
    chip = lax.axis_index("tensor") // CORES
    cols = pl.ds(pl.multiple_of(lax.rem(chip + ring, rings) * wide, 128), wide)
    reads = []
    for part, weight in enumerate(weights):
        reads.append(
            pltpu.make_async_copy(
                weight.at[:, cols], held.at[pl.ds(part * units, units), :], taken.at[part]
            )
        )
        reads[-1].start()
    return reads


def cut_kernel(pieces, gate_ref, up_ref, down_ref, *refs):
    outs, refs = refs[: len(pieces)], refs[len(pieces) :]
    held, (taken, given) = refs[:-2], refs[-2:]
    reads = []
    for place, (which, ring) in enumerate(pieces):
        weights = (gate_ref, up_ref) if which == "up" else (down_ref,)
        reads.append(cut_reads(ring, weights, held[place], taken.at[place]))
    writes = []
    for place, out in enumerate(outs):
        for read in reads[place]:
            read.wait()
        writes.append(pltpu.make_async_copy(held[place], out, given.at[place]))
        writes[-1].start()
    for write in writes:
        write.wait()


def cut(pieces, gate, up, down, wide):
    units = gate.shape[0]
    shapes = [(2 * units if which == "up" else units, wide) for which, _ in pieces]
    whole = pl.BlockSpec(memory_space=pl.ANY)
    return pl.pallas_call(
        lambda *refs: cut_kernel(pieces, *refs),
        out_shape=[jax.ShapeDtypeStruct(shape, BF16) for shape in shapes],
        in_specs=[whole] * 3,
        out_specs=[whole] * len(pieces),
        scratch_shapes=[pltpu.VMEM(shape, BF16) for shape in shapes]
        + [
            pltpu.SemaphoreType.DMA((len(pieces), 2)),
            pltpu.SemaphoreType.DMA((len(pieces),)),
        ],
        name="cut",
    )(gate, up, down)


def half_product(block_ref, rows_ref, half):
    width = rows_ref.shape[1]
    cols = pl.ds(pl.multiple_of(half * width, 128), width)
    return lax.dot_general(
        block_ref[:, cols], rows_ref[...], (((1,), (1,)), ((), ())), preferred_element_type=F32
    )


def near_kernel(rows_ref, *refs):
    *blocks, out_ref = refs
    chip, core = lax.axis_index("tensor") // CORES, lax.rem(lax.axis_index("tensor"), CORES)
    for ring, block in enumerate(blocks):
        source = lax.rem(chip - ring + len(blocks), len(blocks))
        out_ref[source] = half_product(block, rows_ref, core)


def far_kernel(rows_ref, near_ref, *refs):
    *blocks, out_ref = refs
    chip, core = lax.axis_index("tensor") // CORES, lax.rem(lax.axis_index("tensor"), CORES)
    for ring, block in enumerate(blocks):
        source = lax.rem(chip - ring + len(blocks), len(blocks))
        out_ref[source] = (near_ref[source] + half_product(block, rows_ref, 1 - core)).astype(BF16)


def hidden_kernel(partial_ref, out_ref):
    groups, units, _ = out_ref.shape
    act = partial_ref[0].astype(F32)
    for g in range(1, partial_ref.shape[0]):
        act = act + partial_ref[g].astype(F32)
    gate, up = act[:units], act[units:]
    hidden = (jax.nn.silu(gate) * up).astype(BF16)
    for g in range(groups):
        out_ref[g] = hidden


def quarter_kernel(*refs):
    blocks, outs = refs[:-4], refs[-4:]
    core, half = lax.rem(lax.axis_index("tensor"), CORES), lax.axis_index("half")
    units, wide = blocks[0].shape
    width, part = wide // CORES, outs[0].shape[1]
    for (other_half, other_core), out in zip(QUARTERS, outs):
        to_core = lax.rem(core + other_core, CORES)
        to_half = lax.rem(half + other_half, 2)
        start = to_core * width + to_half * (width - part)
        cols = pl.ds(pl.multiple_of(start, 128), part)
        for ring, block in enumerate(blocks):
            out[pl.ds(ring * units, units), :] = block[:, cols]


def down_quarters(blocks, part, groups):
    units, rings = blocks[0].shape[0], len(blocks)
    own, core, pair, both = pl.pallas_call(
        quarter_kernel,
        out_shape=[jax.ShapeDtypeStruct((rings * units, part), BF16)] * 4,
        compiler_params=pltpu.CompilerParams(vmem_limit_bytes=VMEM_BYTES),
        name="quarter",
    )(*blocks)
    swap = shift_pairs(groups, 0, 1)
    across = [(i + h * groups, j + (1 - h) * groups) for h in range(2) for i, j in swap]
    pair = lax.ppermute(pair, "half", [(0, 1), (1, 0)])
    both = lax.ppermute(both, ("half", "tensor"), across)
    core = lax.ppermute(core, "tensor", swap)
    return own, core, pair, both


def down_kernel(hidden_ref, *refs):
    *blocks, out_ref, held = refs
    members, units, _ = hidden_ref.shape
    groups = members // 2
    me, half = lax.axis_index("tensor"), lax.axis_index("half")
    total = None
    for place, (other_half, other_core) in enumerate(QUARTERS):
        from_half = lax.rem(half + other_half, 2)
        for ring in range(groups // CORES):
            source = moved_by(me, groups, ring, other_core, sign=-1)
            held[place, pl.ds(ring * units, units), :] = hidden_ref[
                from_half * groups + source
            ]
        term = lax.dot_general(
            held[place],
            blocks[place][...],
            (((0,), (0,)), ((), ())),
            preferred_element_type=F32,
        )
        total = term if total is None else total + term
    out_ref[...] = total.astype(BF16)


def body(tokens, expert_ids, route_weights, gate_weight, up_weight, down_weight):
    devices_wide = lax.axis_size(EXPERT)
    groups = lax.axis_size("tensor")
    experts = devices_wide // 2
    tok_count, per_token = expert_ids.shape
    width = tokens.shape[1]
    units = gate_weight.shape[1]
    capacity = min(tok_count, tok_count * per_token // experts)
    arrived_count = devices_wide * capacity

    ids = expert_ids.T
    rings, wide = groups // CORES, CORES * width
    gate_up = (gate_weight[0], up_weight[0])
    block = jax.ShapeDtypeStruct((2 * units, wide), BF16)
    whole, held = pl.BlockSpec(memory_space=pl.ANY), pl.BlockSpec(memory_space=pltpu.VMEM)
    packed, across = pl.pallas_call(
        lambda *refs: pack_kernel(2, 2, *refs),
        out_shape=[jax.ShapeDtypeStruct((devices_wide, capacity, width), BF16), block],
        in_specs=[held, held, whole, whole],
        out_specs=[held, whole],
        scratch_shapes=[
            pltpu.VMEM(block.shape, BF16),
            pltpu.SemaphoreType.DMA((2,)),
            pltpu.SemaphoreType.DMA,
        ],
        name="pack",
    )(ids, tokens, *gate_up)
    mix = pl.pallas_call(
        lambda *refs: mix_kernel(capacity, 2, *refs),
        out_shape=jax.ShapeDtypeStruct((arrived_count, tok_count), F32),
        compiler_params=pltpu.CompilerParams(vmem_limit_bytes=VMEM_BYTES),
        name="mix",
    )(ids, route_weights.T)

    pieces = [("up", 1), ("up", 3)] + [("down", ring) for ring in (1, 2, 3)]
    pieces += [("up", 0), ("down", 0)]
    ahead, behind, *down, own, down_own = cut(pieces, *gate_up, down_weight[0], wide)
    blocks = [own, ahead, across, behind]
    down = [down_own, *down]
    for ring in range(1, rings):
        blocks[ring] = lax.ppermute(
            blocks[ring], "tensor", shift_pairs(groups, ring, 0)
        )
        down[ring] = lax.ppermute(down[ring], "tensor", shift_pairs(groups, ring, 0))
    arrived = lax.all_to_all(packed, EXPERT, 0, 0, tiled=True)
    arrived = arrived.reshape(arrived_count, width)
    part = -(-width // 256) * 128
    quarters = down_quarters(down, part, groups)

    partner = lax.ppermute(arrived, "tensor", shift_pairs(groups, 0, 1))
    near = pl.pallas_call(
        near_kernel,
        out_shape=jax.ShapeDtypeStruct((rings, 2 * units, arrived_count), F32),
        compiler_params=pltpu.CompilerParams(vmem_limit_bytes=VMEM_BYTES),
        cost_estimate=pl.CostEstimate(flops=10**9, bytes_accessed=10**6, transcendentals=0),
        name="near",
    )(arrived, *blocks)
    partial = pl.pallas_call(
        far_kernel,
        out_shape=jax.ShapeDtypeStruct((rings, 2 * units, arrived_count), BF16),
        compiler_params=pltpu.CompilerParams(vmem_limit_bytes=VMEM_BYTES),
        name="far",
    )(partner, near, *blocks)
    same_core = [list(range(core, groups, CORES)) for core in range(CORES)]
    partial = lax.all_to_all(
        partial, "tensor", 0, 0, axis_index_groups=same_core, tiled=True
    )
    hidden = pl.pallas_call(
        hidden_kernel,
        out_shape=jax.ShapeDtypeStruct((2 * groups, units, arrived_count), BF16),
        compiler_params=pltpu.CompilerParams(vmem_limit_bytes=VMEM_BYTES),
        name="hidden",
    )(partial)
    hidden, mix = lax.optimization_barrier((hidden, mix))
    hidden = lax.all_to_all(hidden, ("half", "tensor"), 0, 0, tiled=True)
    half_out = pl.pallas_call(
        down_kernel,
        out_shape=jax.ShapeDtypeStruct((arrived_count, part), BF16),
        scratch_shapes=[pltpu.VMEM((4, rings * units, arrived_count), BF16)],
        compiler_params=pltpu.CompilerParams(vmem_limit_bytes=VMEM_BYTES),
        name="down",
    )(hidden, *quarters)
    returned = lax.all_to_all(
        half_out.reshape(devices_wide, capacity, part), EXPERT, 0, 0, tiled=True
    ).reshape(arrived_count, part)
    return pl.pallas_call(
        lambda *refs: combine_kernel(capacity, *refs),
        out_shape=jax.ShapeDtypeStruct((tok_count, width), BF16),
        compiler_params=pltpu.CompilerParams(vmem_limit_bytes=VMEM_BYTES),
        name="combine",
    )(mix, returned)


def solution(mesh):
    wide, groups = mesh.devices.shape
    mesh = Mesh(mesh.devices.reshape(wide // 2, 2, groups), (*EXPERT, "tensor"))
    placed = (
        P(EXPERT, "tensor"),
        P(EXPERT, None),
        P(EXPERT, None),
        P(EXPERT, "tensor", None),
        P(EXPERT, "tensor", None),
        P(EXPERT, "tensor", None),
    )

    def step(*args):
        return body(*args)

    step = jax.shard_map(
        step, mesh=mesh, in_specs=placed, out_specs=P(EXPERT, "tensor"), check_vma=False
    )
    return step
```

```python
import jax
import jax.numpy as jnp
from jax import lax
from jax.experimental import pallas as pl
from jax.experimental.pallas import tpu as pltpu
from jax.sharding import PartitionSpec as P

F32 = jnp.float32
BF16 = jnp.bfloat16


def slot_onehot(ids, slots, capacity, copies):
    per_token, tok_count = ids.shape
    slot = lax.broadcasted_iota(jnp.int32, (slots, tok_count), 0)
    expert = slot // (capacity * copies)
    hit = jnp.zeros((slots, tok_count), F32)
    for j in range(per_token):
        hit = hit + jnp.where(ids[j : j + 1, :] == expert, 1.0, 0.0)
    row = lax.broadcasted_iota(jnp.int32, (tok_count, tok_count), 0)
    col = lax.broadcasted_iota(jnp.int32, (tok_count, tok_count), 1)
    before = jnp.where(row < col, 1.0, 0.0).astype(BF16)
    earlier = jnp.dot(hit.astype(BF16), before, preferred_element_type=F32)
    rank = (slot % capacity).astype(F32)
    return jnp.where((hit > 0.5) & (earlier == rank), 1.0, 0.0), expert


def pack_kernel(copies, ring, ids_ref, tok_ref, gate_ref, up_ref, out_ref, block_ref, *refs):
    ids, tok, packed, held, taken, given, small = refs
    fetches = [
        pltpu.make_async_copy(ids_ref, ids, small.at[0]),
        pltpu.make_async_copy(tok_ref, tok, small.at[1]),
    ]
    for fetch in fetches:
        fetch.start()
    reads = cut_reads(ring, (gate_ref, up_ref), held, taken)
    peers, capacity, width = packed.shape
    for fetch in fetches:
        fetch.wait()
    select, _ = slot_onehot(ids[...], peers * capacity, capacity, copies)
    rows = jnp.dot(select.astype(BF16), tok[...], preferred_element_type=F32)
    packed[...] = rows.reshape(peers, capacity, width).astype(BF16)
    for read in reads:
        read.wait()
    writes = [
        pltpu.make_async_copy(held, block_ref, given.at[0]),
        pltpu.make_async_copy(packed, out_ref, given.at[1]),
    ]
    for write in writes:
        write.start()
    for write in writes:
        write.wait()


def mix_kernel(capacity, copies, ids_ref, route_ref, mix_ref):
    ids = ids_ref[...]
    route = route_ref[...]
    select, expert = slot_onehot(ids, mix_ref.shape[0], capacity, copies)
    weight = jnp.zeros(select.shape, F32)
    for j in range(ids.shape[0]):
        weight = weight + jnp.where(ids[j : j + 1, :] == expert, route[j : j + 1, :], 0.0)
    mix_ref[...] = select * weight


def combine_kernel(mix_ref, rows_ref, out_ref):
    mix = mix_ref[...]
    high = mix.astype(BF16)
    low = (mix - high.astype(F32)).astype(BF16)
    rows = rows_ref[...]
    dims = (((0,), (0,)), ((), ()))
    total = lax.dot_general(high, rows, dims, preferred_element_type=F32)
    total = total + lax.dot_general(low, rows, dims, preferred_element_type=F32)
    out_ref[...] = total.astype(BF16)


CORES = 2
VMEM_BYTES = 10 * 2**20


def moved_by(index, groups, ring, core, sign=1):
    rings = groups // CORES
    place = lax.rem(index // CORES + sign * ring + rings, rings)
    return place * CORES + lax.rem(lax.rem(index, CORES) + core, CORES)


def shift_pairs(groups, ring, core):
    rings = groups // CORES
    return [
        (i, (i // CORES + ring) % rings * CORES + (i + core) % CORES) for i in range(groups)
    ]


def cut_reads(ring, weights, held, taken):
    wide = held.shape[1]
    units, full = weights[0].shape
    rings = full // wide
    chip = lax.axis_index("tensor") // CORES
    cols = pl.ds(pl.multiple_of(lax.rem(chip + ring, rings) * wide, 128), wide)
    reads = []
    for part, weight in enumerate(weights):
        reads.append(
            pltpu.make_async_copy(
                weight.at[:, cols], held.at[pl.ds(part * units, units), :], taken.at[part]
            )
        )
        reads[-1].start()
    return reads


def cut_kernel(rings, parts, *refs):
    weights, refs = refs[:parts], refs[parts:]
    *outs, held, taken, given = refs
    reads = [
        cut_reads(ring, weights, held.at[place], taken.at[place])
        for place, ring in enumerate(rings)
    ]
    writes = []
    for place, out in enumerate(outs):
        for read in reads[place]:
            read.wait()
        writes.append(pltpu.make_async_copy(held.at[place], out, given.at[place]))
        writes[-1].start()
    for write in writes:
        write.wait()


def cut(rings, weights, wide):
    parts, units = len(weights), weights[0].shape[0]
    shape = jax.ShapeDtypeStruct((parts * units, wide), BF16)
    whole = pl.BlockSpec(memory_space=pl.ANY)
    return pl.pallas_call(
        lambda *refs: cut_kernel(rings, parts, *refs),
        out_shape=[shape] * len(rings),
        in_specs=[whole] * parts,
        out_specs=[whole] * len(rings),
        scratch_shapes=[
            pltpu.VMEM((len(rings), *shape.shape), BF16),
            pltpu.SemaphoreType.DMA((len(rings), parts)),
            pltpu.SemaphoreType.DMA((len(rings),)),
        ],
        name="cut",
    )(*weights)


def gate_up_kernel(rows_ref, *refs):
    *blocks, out_ref = refs
    rings, width = len(blocks), rows_ref.shape[2]
    chip = lax.axis_index("tensor") // CORES
    dims = (((1,), (1,)), ((), ()))
    for ring, block in enumerate(blocks):
        total = None
        for core in range(CORES):
            term = lax.dot_general(
                block[:, core * width : (core + 1) * width],
                rows_ref[core],
                dims,
                preferred_element_type=F32,
            )
            total = term if total is None else total + term
        out_ref[lax.rem(chip - ring + rings, rings)] = total.astype(BF16)


def hidden_kernel(partial_ref, out_ref):
    groups, units, _ = out_ref.shape
    act = partial_ref[0].astype(F32)
    for g in range(1, partial_ref.shape[0]):
        act = act + partial_ref[g].astype(F32)
    gate, up = act[:units], act[units:]
    hidden = (jax.nn.silu(gate) * up).astype(BF16)
    for g in range(groups):
        out_ref[g] = hidden


def core_cut_kernel(*refs):
    *blocks, near_ref, far_ref = refs
    core = lax.rem(lax.axis_index("tensor"), CORES)
    units = blocks[0].shape[0]
    width = near_ref.shape[1]
    for ring, block in enumerate(blocks):
        rows = pl.ds(ring * units, units)
        near_ref[rows, :] = block[:, pl.ds(pl.multiple_of(core * width, 128), width)]
        far_ref[rows, :] = block[:, pl.ds(pl.multiple_of((1 - core) * width, 128), width)]


def down_columns(weight, width, groups):
    units = weight.shape[0]
    rings = groups // CORES
    order = (1, 2, 3, 0)
    cuts = cut(order, (weight,), CORES * width)
    blocks = dict(zip(order, cuts))
    for ring in range(1, rings):
        blocks[ring] = lax.ppermute(
            blocks[ring], "tensor", shift_pairs(groups, ring, 0)
        )
    near, far = pl.pallas_call(
        core_cut_kernel,
        out_shape=[jax.ShapeDtypeStruct((rings * units, width), BF16)] * 2,
        compiler_params=pltpu.CompilerParams(vmem_limit_bytes=VMEM_BYTES),
        name="core_cut",
    )(*[blocks[ring] for ring in range(rings)])
    return near, lax.ppermute(far, "tensor", shift_pairs(groups, 0, 1))


def down_kernel(hidden_ref, near_ref, far_ref, keep_ref, give_ref, held, rows):
    groups, units, _ = hidden_ref.shape
    me = lax.axis_index("tensor")
    for core in range(CORES):
        for ring in range(groups // CORES):
            source = moved_by(me, groups, ring, core, sign=-1)
            held[core, pl.ds(ring * units, units), :] = hidden_ref[source]
    dims = (((0,), (0,)), ((), ()))
    total = lax.dot_general(held[0], near_ref[...], dims, preferred_element_type=F32)
    total = total + lax.dot_general(held[1], far_ref[...], dims, preferred_element_type=F32)
    rows[...] = total.reshape(rows.shape)
    slots = keep_ref.shape[1]
    half = lax.rem(lax.axis_index("expert"), 2)
    low, high = rows[:, :slots, :], rows[:, slots:, :]
    keep_ref[...] = jnp.where(half == 0, low, high).astype(BF16)
    give_ref[...] = jnp.where(half == 0, high, low).astype(BF16)


def body(tokens, expert_ids, route_weights, gate_weight, up_weight, down_weight):
    devices_wide = lax.axis_size("expert")
    groups = lax.axis_size("tensor")
    experts = devices_wide // 2
    tok_count, per_token = expert_ids.shape
    width = tokens.shape[1]
    units = gate_weight.shape[1]
    capacity = min(tok_count, tok_count * per_token // experts)
    arrived_count = devices_wide * capacity

    ids = expert_ids.T
    rings, wide = groups // CORES, CORES * width
    gate_up = (gate_weight[0], up_weight[0])
    part = jax.ShapeDtypeStruct((2 * units, wide), BF16)
    whole = pl.BlockSpec(memory_space=pl.ANY)
    packed, across = pl.pallas_call(
        lambda *refs: pack_kernel(2, 2, *refs),
        out_shape=[jax.ShapeDtypeStruct((devices_wide, capacity, width), BF16), part],
        in_specs=[whole] * 4,
        out_specs=[whole] * 2,
        scratch_shapes=[
            pltpu.VMEM(ids.shape, jnp.int32),
            pltpu.VMEM(tokens.shape, BF16),
            pltpu.VMEM((devices_wide, capacity, width), BF16),
            pltpu.VMEM(part.shape, BF16),
            pltpu.SemaphoreType.DMA((2,)),
            pltpu.SemaphoreType.DMA((2,)),
            pltpu.SemaphoreType.DMA((2,)),
        ],
        name="pack",
    )(ids, tokens, *gate_up)
    mix = pl.pallas_call(
        lambda *refs: mix_kernel(capacity, 1, *refs),
        out_shape=jax.ShapeDtypeStruct((experts * capacity, tok_count), F32),
        compiler_params=pltpu.CompilerParams(vmem_limit_bytes=VMEM_BYTES),
        name="mix",
    )(ids, route_weights.T)

    ahead, behind, own = cut((1, 3, 0), gate_up, wide)
    blocks = [own, ahead, across, behind]
    for ring in range(1, rings):
        blocks[ring] = lax.ppermute(
            blocks[ring], "tensor", shift_pairs(groups, ring, 0)
        )
    arrived = lax.all_to_all(packed, "expert", 0, 0, tiled=True)
    arrived = arrived.reshape(arrived_count, width)
    down_near, down_far = down_columns(down_weight[0], width, groups)

    arrived, *blocks = lax.optimization_barrier((arrived, *blocks))
    one_chip = [[chip * CORES + core for core in range(CORES)] for chip in range(rings)]
    rows = lax.all_to_all(
        jnp.broadcast_to(arrived, (CORES, *arrived.shape)),
        "tensor",
        0,
        0,
        axis_index_groups=one_chip,
        tiled=True,
    )
    partial = pl.pallas_call(
        gate_up_kernel,
        out_shape=jax.ShapeDtypeStruct((rings, 2 * units, arrived_count), BF16),
        compiler_params=pltpu.CompilerParams(vmem_limit_bytes=VMEM_BYTES),
        name="gate_up",
    )(rows, *blocks)
    same_core = [list(range(core, groups, CORES)) for core in range(CORES)]
    partial = lax.all_to_all(
        partial, "tensor", 0, 0, axis_index_groups=same_core, tiled=True
    )
    hidden = pl.pallas_call(
        hidden_kernel,
        out_shape=jax.ShapeDtypeStruct((groups, units, arrived_count), BF16),
        compiler_params=pltpu.CompilerParams(vmem_limit_bytes=VMEM_BYTES),
        name="hidden",
    )(partial)
    hidden, mix = lax.optimization_barrier((hidden, mix))
    hidden = lax.all_to_all(hidden, "tensor", 0, 0, tiled=True)
    slots = capacity // 2
    kept, given = pl.pallas_call(
        down_kernel,
        out_shape=[jax.ShapeDtypeStruct((devices_wide, slots, width), BF16)] * 2,
        scratch_shapes=[
            pltpu.VMEM((2, groups // 2 * units, arrived_count), BF16),
            pltpu.VMEM((devices_wide, capacity, width), F32),
        ],
        compiler_params=pltpu.CompilerParams(vmem_limit_bytes=VMEM_BYTES),
        name="down",
    )(hidden, down_near, down_far)
    pairs = [(i, i + 1 - 2 * (i % 2)) for i in range(devices_wide)]
    taken = lax.ppermute(given, "expert", pairs)
    both = (kept.astype(F32) + taken.astype(F32)).astype(BF16)
    returned = lax.all_to_all(both, "expert", 0, 0, tiled=True)
    returned = returned.reshape(devices_wide * slots, width)
    return pl.pallas_call(
        combine_kernel,
        out_shape=jax.ShapeDtypeStruct((tok_count, width), BF16),
        compiler_params=pltpu.CompilerParams(vmem_limit_bytes=VMEM_BYTES),
        name="combine",
    )(mix, returned)


def solution(mesh):
    placed = (
        P("expert", "tensor"),
        P("expert", None),
        P("expert", None),
        P("expert", "tensor", None),
        P("expert", "tensor", None),
        P("expert", "tensor", None),
    )
    def step(*args):
        return body(*args)

    step = jax.shard_map(
        step, mesh=mesh, in_specs=placed, out_specs=P("expert", "tensor"), check_vma=False
    )
    return step
```

```python
import jax
import jax.numpy as jnp
from jax import lax
from jax.experimental import pallas as pl
from jax.experimental.pallas import tpu as pltpu
from jax.sharding import PartitionSpec as P

F32 = jnp.float32
BF16 = jnp.bfloat16


def slot_onehot(ids, slots, capacity, copies):
    per_token, tok_count = ids.shape
    slot = lax.broadcasted_iota(jnp.int32, (slots, tok_count), 0)
    expert = slot // (capacity * copies)
    hit = jnp.zeros((slots, tok_count), F32)
    for j in range(per_token):
        hit = hit + jnp.where(ids[j : j + 1, :] == expert, 1.0, 0.0)
    row = lax.broadcasted_iota(jnp.int32, (tok_count, tok_count), 0)
    col = lax.broadcasted_iota(jnp.int32, (tok_count, tok_count), 1)
    before = jnp.where(row < col, 1.0, 0.0).astype(BF16)
    earlier = jnp.dot(hit.astype(BF16), before, preferred_element_type=F32)
    rank = (slot % capacity).astype(F32)
    return jnp.where((hit > 0.5) & (earlier == rank), 1.0, 0.0), expert


def pack_kernel(copies, ring, ids_ref, tok_ref, gate_ref, up_ref, out_ref, block_ref, *refs):
    ids, tok, packed, held, taken, given, small = refs
    fetches = [
        pltpu.make_async_copy(ids_ref, ids, small.at[0]),
        pltpu.make_async_copy(tok_ref, tok, small.at[1]),
    ]
    for fetch in fetches:
        fetch.start()
    reads = cut_reads(ring, (gate_ref, up_ref), held, taken)
    peers, capacity, width = packed.shape
    for fetch in fetches:
        fetch.wait()
    select, _ = slot_onehot(ids[...], peers * capacity, capacity, copies)
    rows = jnp.dot(select.astype(BF16), tok[...], preferred_element_type=F32)
    packed[...] = rows.reshape(peers, capacity, width).astype(BF16)
    for read in reads:
        read.wait()
    writes = [
        pltpu.make_async_copy(held, block_ref, given.at[0]),
        pltpu.make_async_copy(packed, out_ref, given.at[1]),
    ]
    for write in writes:
        write.start()
    for write in writes:
        write.wait()


def mix_kernel(capacity, copies, ids_ref, route_ref, mix_ref):
    ids = ids_ref[...]
    route = route_ref[...]
    select, expert = slot_onehot(ids, mix_ref.shape[0], capacity, copies)
    weight = jnp.zeros(select.shape, F32)
    for j in range(ids.shape[0]):
        weight = weight + jnp.where(ids[j : j + 1, :] == expert, route[j : j + 1, :], 0.0)
    mix_ref[...] = select * weight


def combine_kernel(mix_ref, rows_ref, out_ref):
    mix = mix_ref[...]
    high = mix.astype(BF16)
    low = (mix - high.astype(F32)).astype(BF16)
    rows = rows_ref[...]
    dims = (((0,), (0,)), ((), ()))
    total = lax.dot_general(high, rows, dims, preferred_element_type=F32)
    total = total + lax.dot_general(low, rows, dims, preferred_element_type=F32)
    out_ref[...] = total.astype(BF16)


CORES = 2
VMEM_BYTES = 10 * 2**20


def moved_by(index, groups, ring, core, sign=1):
    rings = groups // CORES
    place = lax.rem(index // CORES + sign * ring + rings, rings)
    return place * CORES + lax.rem(lax.rem(index, CORES) + core, CORES)


def shift_pairs(groups, ring, core):
    rings = groups // CORES
    return [
        (i, (i // CORES + ring) % rings * CORES + (i + core) % CORES) for i in range(groups)
    ]


def cut_reads(ring, weights, held, taken):
    wide = held.shape[1]
    units, full = weights[0].shape
    rings = full // wide
    chip = lax.axis_index("tensor") // CORES
    cols = pl.ds(pl.multiple_of(lax.rem(chip + ring, rings) * wide, 128), wide)
    reads = []
    for part, weight in enumerate(weights):
        reads.append(
            pltpu.make_async_copy(
                weight.at[:, cols], held.at[pl.ds(part * units, units), :], taken.at[part]
            )
        )
        reads[-1].start()
    return reads


def cut_kernel(pieces, gate_ref, up_ref, down_ref, *refs):
    outs, refs = refs[: len(pieces)], refs[len(pieces) :]
    held, (taken, given) = refs[:-2], refs[-2:]
    reads = []
    for place, (which, ring) in enumerate(pieces):
        weights = (gate_ref, up_ref) if which == "up" else (down_ref,)
        reads.append(cut_reads(ring, weights, held[place], taken.at[place]))
    writes = []
    for place, out in enumerate(outs):
        for read in reads[place]:
            read.wait()
        writes.append(pltpu.make_async_copy(held[place], out, given.at[place]))
        writes[-1].start()
    for write in writes:
        write.wait()


def cut(pieces, gate, up, down, wide):
    units = gate.shape[0]
    shapes = [(2 * units if which == "up" else units, wide) for which, _ in pieces]
    whole = pl.BlockSpec(memory_space=pl.ANY)
    return pl.pallas_call(
        lambda *refs: cut_kernel(pieces, *refs),
        out_shape=[jax.ShapeDtypeStruct(shape, BF16) for shape in shapes],
        in_specs=[whole] * 3,
        out_specs=[whole] * len(pieces),
        scratch_shapes=[pltpu.VMEM(shape, BF16) for shape in shapes]
        + [
            pltpu.SemaphoreType.DMA((len(pieces), 2)),
            pltpu.SemaphoreType.DMA((len(pieces),)),
        ],
        name="cut",
    )(gate, up, down)


def half_product(block_ref, rows_ref, half):
    width = rows_ref.shape[1]
    cols = pl.ds(pl.multiple_of(half * width, 128), width)
    return lax.dot_general(
        block_ref[:, cols], rows_ref[...], (((1,), (1,)), ((), ())), preferred_element_type=F32
    )


def near_kernel(rows_ref, *refs):
    *blocks, out_ref = refs
    chip, core = lax.axis_index("tensor") // CORES, lax.rem(lax.axis_index("tensor"), CORES)
    for ring, block in enumerate(blocks):
        source = lax.rem(chip - ring + len(blocks), len(blocks))
        out_ref[source] = half_product(block, rows_ref, core)


def far_kernel(rows_ref, near_ref, *refs):
    *blocks, out_ref = refs
    chip, core = lax.axis_index("tensor") // CORES, lax.rem(lax.axis_index("tensor"), CORES)
    for ring, block in enumerate(blocks):
        source = lax.rem(chip - ring + len(blocks), len(blocks))
        out_ref[source] = (near_ref[source] + half_product(block, rows_ref, 1 - core)).astype(BF16)


def hidden_kernel(partial_ref, out_ref):
    groups, units, _ = out_ref.shape
    act = partial_ref[0].astype(F32)
    for g in range(1, partial_ref.shape[0]):
        act = act + partial_ref[g].astype(F32)
    gate, up = act[:units], act[units:]
    hidden = (jax.nn.silu(gate) * up).astype(BF16)
    for g in range(groups):
        out_ref[g] = hidden


def core_cut_kernel(*refs):
    *blocks, near_ref, far_ref = refs
    core = lax.rem(lax.axis_index("tensor"), CORES)
    units = blocks[0].shape[0]
    width = near_ref.shape[1]
    for ring, block in enumerate(blocks):
        rows = pl.ds(ring * units, units)
        near_ref[rows, :] = block[:, pl.ds(pl.multiple_of(core * width, 128), width)]
        far_ref[rows, :] = block[:, pl.ds(pl.multiple_of((1 - core) * width, 128), width)]


def down_columns(blocks, width, groups):
    units, rings = blocks[0].shape[0], len(blocks)
    for ring in range(1, rings):
        blocks[ring] = lax.ppermute(
            blocks[ring], "tensor", shift_pairs(groups, ring, 0)
        )
    near, far = pl.pallas_call(
        core_cut_kernel,
        out_shape=[jax.ShapeDtypeStruct((rings * units, width), BF16)] * 2,
        compiler_params=pltpu.CompilerParams(vmem_limit_bytes=VMEM_BYTES),
        name="core_cut",
    )(*[blocks[ring] for ring in range(rings)])
    return near, lax.ppermute(far, "tensor", shift_pairs(groups, 0, 1))


def down_kernel(hidden_ref, near_ref, far_ref, keep_ref, give_ref, held, rows):
    groups, units, _ = hidden_ref.shape
    me = lax.axis_index("tensor")
    for core in range(CORES):
        for ring in range(groups // CORES):
            source = moved_by(me, groups, ring, core, sign=-1)
            held[core, pl.ds(ring * units, units), :] = hidden_ref[source]
    dims = (((0,), (0,)), ((), ()))
    total = lax.dot_general(held[0], near_ref[...], dims, preferred_element_type=F32)
    total = total + lax.dot_general(held[1], far_ref[...], dims, preferred_element_type=F32)
    rows[...] = total.reshape(rows.shape)
    slots = keep_ref.shape[1]
    half = lax.rem(lax.axis_index("expert"), 2)
    low, high = rows[:, :slots, :], rows[:, slots:, :]
    keep_ref[...] = jnp.where(half == 0, low, high).astype(BF16)
    give_ref[...] = jnp.where(half == 0, high, low).astype(BF16)


def body(tokens, expert_ids, route_weights, gate_weight, up_weight, down_weight):
    devices_wide = lax.axis_size("expert")
    groups = lax.axis_size("tensor")
    experts = devices_wide // 2
    tok_count, per_token = expert_ids.shape
    width = tokens.shape[1]
    units = gate_weight.shape[1]
    capacity = min(tok_count, tok_count * per_token // experts)
    arrived_count = devices_wide * capacity

    ids = expert_ids.T
    rings, wide = groups // CORES, CORES * width
    gate_up = (gate_weight[0], up_weight[0])
    part = jax.ShapeDtypeStruct((2 * units, wide), BF16)
    whole = pl.BlockSpec(memory_space=pl.ANY)
    packed, across = pl.pallas_call(
        lambda *refs: pack_kernel(2, 2, *refs),
        out_shape=[jax.ShapeDtypeStruct((devices_wide, capacity, width), BF16), part],
        in_specs=[whole] * 4,
        out_specs=[whole] * 2,
        scratch_shapes=[
            pltpu.VMEM(ids.shape, jnp.int32),
            pltpu.VMEM(tokens.shape, BF16),
            pltpu.VMEM((devices_wide, capacity, width), BF16),
            pltpu.VMEM(part.shape, BF16),
            pltpu.SemaphoreType.DMA((2,)),
            pltpu.SemaphoreType.DMA((2,)),
            pltpu.SemaphoreType.DMA((2,)),
        ],
        name="pack",
    )(ids, tokens, *gate_up)
    mix = pl.pallas_call(
        lambda *refs: mix_kernel(capacity, 1, *refs),
        out_shape=jax.ShapeDtypeStruct((experts * capacity, tok_count), F32),
        compiler_params=pltpu.CompilerParams(vmem_limit_bytes=VMEM_BYTES),
        name="mix",
    )(ids, route_weights.T)

    ahead, behind = cut([("up", 1), ("up", 3)], *gate_up, down_weight[0], wide)
    pieces = [("down", ring) for ring in (1, 2, 3)] + [("up", 0), ("down", 0)]
    *down, own, down_own = cut(pieces, *gate_up, down_weight[0], wide)
    blocks = [own, ahead, across, behind]
    for ring in range(1, rings):
        blocks[ring] = lax.ppermute(
            blocks[ring], "tensor", shift_pairs(groups, ring, 0)
        )
    arrived = lax.all_to_all(packed, "expert", 0, 0, tiled=True)
    arrived = arrived.reshape(arrived_count, width)
    arrived, mix = lax.optimization_barrier((arrived, mix))
    down_near, down_far = down_columns([down_own, *down], width, groups)

    partner = lax.ppermute(arrived, "tensor", shift_pairs(groups, 0, 1))
    near = pl.pallas_call(
        near_kernel,
        out_shape=jax.ShapeDtypeStruct((rings, 2 * units, arrived_count), F32),
        compiler_params=pltpu.CompilerParams(vmem_limit_bytes=VMEM_BYTES),
        cost_estimate=pl.CostEstimate(flops=10**9, bytes_accessed=10**6, transcendentals=0),
        name="near",
    )(arrived, *blocks)
    partial = pl.pallas_call(
        far_kernel,
        out_shape=jax.ShapeDtypeStruct((rings, 2 * units, arrived_count), BF16),
        compiler_params=pltpu.CompilerParams(vmem_limit_bytes=VMEM_BYTES),
        name="far",
    )(partner, near, *blocks)
    same_core = [list(range(core, groups, CORES)) for core in range(CORES)]
    partial = lax.all_to_all(
        partial, "tensor", 0, 0, axis_index_groups=same_core, tiled=True
    )
    hidden = pl.pallas_call(
        hidden_kernel,
        out_shape=jax.ShapeDtypeStruct((groups, units, arrived_count), BF16),
        compiler_params=pltpu.CompilerParams(vmem_limit_bytes=VMEM_BYTES),
        name="hidden",
    )(partial)
    hidden = lax.all_to_all(hidden, "tensor", 0, 0, tiled=True)
    slots = capacity // 2
    kept, given = pl.pallas_call(
        down_kernel,
        out_shape=[jax.ShapeDtypeStruct((devices_wide, slots, width), BF16)] * 2,
        scratch_shapes=[
            pltpu.VMEM((2, groups // 2 * units, arrived_count), BF16),
            pltpu.VMEM((devices_wide, capacity, width), F32),
        ],
        compiler_params=pltpu.CompilerParams(vmem_limit_bytes=VMEM_BYTES),
        name="down",
    )(hidden, down_near, down_far)
    pairs = [(i, i + 1 - 2 * (i % 2)) for i in range(devices_wide)]
    taken = lax.ppermute(given, "expert", pairs)
    both = (kept.astype(F32) + taken.astype(F32)).astype(BF16)
    returned = lax.all_to_all(both, "expert", 0, 0, tiled=True)
    returned = returned.reshape(devices_wide * slots, width)
    return pl.pallas_call(
        combine_kernel,
        out_shape=jax.ShapeDtypeStruct((tok_count, width), BF16),
        compiler_params=pltpu.CompilerParams(vmem_limit_bytes=VMEM_BYTES),
        name="combine",
    )(mix, returned)


def solution(mesh):
    placed = (
        P("expert", "tensor"),
        P("expert", None),
        P("expert", None),
        P("expert", "tensor", None),
        P("expert", "tensor", None),
        P("expert", "tensor", None),
    )
    def step(*args):
        return body(*args)

    step = jax.shard_map(
        step, mesh=mesh, in_specs=placed, out_specs=P("expert", "tensor"), check_vma=False
    )
    return step
```

```python
import jax
import jax.numpy as jnp
from jax import lax
from jax.experimental import pallas as pl
from jax.experimental.pallas import tpu as pltpu
from jax.sharding import PartitionSpec as P

F32 = jnp.float32
BF16 = jnp.bfloat16


def slot_onehot(ids, slots, capacity, copies):
    per_token, tok_count = ids.shape
    slot = lax.broadcasted_iota(jnp.int32, (slots, tok_count), 0)
    expert = slot // (capacity * copies)
    hit = jnp.zeros((slots, tok_count), F32)
    for j in range(per_token):
        hit = hit + jnp.where(ids[j : j + 1, :] == expert, 1.0, 0.0)
    row = lax.broadcasted_iota(jnp.int32, (tok_count, tok_count), 0)
    col = lax.broadcasted_iota(jnp.int32, (tok_count, tok_count), 1)
    before = jnp.where(row < col, 1.0, 0.0).astype(BF16)
    earlier = jnp.dot(hit.astype(BF16), before, preferred_element_type=F32)
    rank = (slot % capacity).astype(F32)
    return jnp.where((hit > 0.5) & (earlier == rank), 1.0, 0.0), expert


def pack_kernel(copies, ring, ids_ref, tok_ref, gate_ref, up_ref, out_ref, block_ref, *refs):
    ids, tok, packed, held, taken, given, small = refs
    fetches = [
        pltpu.make_async_copy(ids_ref, ids, small.at[0]),
        pltpu.make_async_copy(tok_ref, tok, small.at[1]),
    ]
    for fetch in fetches:
        fetch.start()
    reads = cut_reads(ring, (gate_ref, up_ref), held, taken)
    peers, capacity, width = packed.shape
    for fetch in fetches:
        fetch.wait()
    select, _ = slot_onehot(ids[...], peers * capacity, capacity, copies)
    rows = jnp.dot(select.astype(BF16), tok[...], preferred_element_type=F32)
    packed[...] = rows.reshape(peers, capacity, width).astype(BF16)
    for read in reads:
        read.wait()
    writes = [
        pltpu.make_async_copy(held, block_ref, given.at[0]),
        pltpu.make_async_copy(packed, out_ref, given.at[1]),
    ]
    for write in writes:
        write.start()
    for write in writes:
        write.wait()


def mix_kernel(capacity, copies, ids_ref, route_ref, mix_ref):
    ids = ids_ref[...]
    route = route_ref[...]
    select, expert = slot_onehot(ids, mix_ref.shape[0], capacity, copies)
    weight = jnp.zeros(select.shape, F32)
    for j in range(ids.shape[0]):
        weight = weight + jnp.where(ids[j : j + 1, :] == expert, route[j : j + 1, :], 0.0)
    mix_ref[...] = select * weight


def combine_kernel(mix_ref, rows_ref, out_ref):
    mix = mix_ref[...]
    high = mix.astype(BF16)
    low = (mix - high.astype(F32)).astype(BF16)
    rows = rows_ref[...]
    dims = (((0,), (0,)), ((), ()))
    total = lax.dot_general(high, rows, dims, preferred_element_type=F32)
    total = total + lax.dot_general(low, rows, dims, preferred_element_type=F32)
    out_ref[...] = total.astype(BF16)


CORES = 2
VMEM_BYTES = 10 * 2**20


def moved_by(index, groups, ring, core, sign=1):
    rings = groups // CORES
    place = lax.rem(index // CORES + sign * ring + rings, rings)
    return place * CORES + lax.rem(lax.rem(index, CORES) + core, CORES)


def shift_pairs(groups, ring, core):
    rings = groups // CORES
    return [
        (i, (i // CORES + ring) % rings * CORES + (i + core) % CORES) for i in range(groups)
    ]


def cut_reads(ring, weights, held, taken):
    wide = held.shape[1]
    units, full = weights[0].shape
    rings = full // wide
    chip = lax.axis_index("tensor") // CORES
    cols = pl.ds(pl.multiple_of(lax.rem(chip + ring, rings) * wide, 128), wide)
    reads = []
    for part, weight in enumerate(weights):
        reads.append(
            pltpu.make_async_copy(
                weight.at[:, cols], held.at[pl.ds(part * units, units), :], taken.at[part]
            )
        )
        reads[-1].start()
    return reads


def cut_kernel(pieces, gate_ref, up_ref, down_ref, *refs):
    outs, refs = refs[: len(pieces)], refs[len(pieces) :]
    held, (taken, given) = refs[:-2], refs[-2:]
    reads = []
    for place, (which, ring) in enumerate(pieces):
        weights = (gate_ref, up_ref) if which == "up" else (down_ref,)
        reads.append(cut_reads(ring, weights, held[place], taken.at[place]))
    writes = []
    for place, out in enumerate(outs):
        for read in reads[place]:
            read.wait()
        writes.append(pltpu.make_async_copy(held[place], out, given.at[place]))
        writes[-1].start()
    for write in writes:
        write.wait()


def cut(pieces, gate, up, down, wide):
    units = gate.shape[0]
    shapes = [(2 * units if which == "up" else units, wide) for which, _ in pieces]
    whole = pl.BlockSpec(memory_space=pl.ANY)
    return pl.pallas_call(
        lambda *refs: cut_kernel(pieces, *refs),
        out_shape=[jax.ShapeDtypeStruct(shape, BF16) for shape in shapes],
        in_specs=[whole] * 3,
        out_specs=[whole] * len(pieces),
        scratch_shapes=[pltpu.VMEM(shape, BF16) for shape in shapes]
        + [
            pltpu.SemaphoreType.DMA((len(pieces), 2)),
            pltpu.SemaphoreType.DMA((len(pieces),)),
        ],
        name="cut",
    )(gate, up, down)


def half_product(block_ref, rows_ref, half):
    width = rows_ref.shape[1]
    cols = pl.ds(pl.multiple_of(half * width, 128), width)
    return lax.dot_general(
        block_ref[:, cols], rows_ref[...], (((1,), (1,)), ((), ())), preferred_element_type=F32
    )


def near_kernel(rows_ref, *refs):
    *blocks, out_ref = refs
    chip, core = lax.axis_index("tensor") // CORES, lax.rem(lax.axis_index("tensor"), CORES)
    for ring, block in enumerate(blocks):
        source = lax.rem(chip - ring + len(blocks), len(blocks))
        out_ref[source] = half_product(block, rows_ref, core)


def far_kernel(rows_ref, near_ref, *refs):
    *blocks, out_ref, held, given = refs
    rings = len(blocks)
    chip, core = lax.axis_index("tensor") // CORES, lax.rem(lax.axis_index("tensor"), CORES)
    writes = []
    for ring, block in enumerate(blocks):
        source = lax.rem(chip - ring + rings, rings)
        total = near_ref[source] + half_product(block, rows_ref, 1 - core)
        held[ring] = total.astype(BF16)
        writes.append(pltpu.make_async_copy(held.at[ring], out_ref.at[source], given.at[ring]))
        writes[-1].start()
    for write in writes:
        write.wait()


def hidden_kernel(partial_ref, out_ref):
    groups, units, _ = out_ref.shape
    act = partial_ref[0].astype(F32)
    for g in range(1, partial_ref.shape[0]):
        act = act + partial_ref[g].astype(F32)
    gate, up = act[:units], act[units:]
    hidden = (jax.nn.silu(gate) * up).astype(BF16)
    for g in range(groups):
        out_ref[g] = hidden


def core_cut_kernel(*refs):
    *blocks, near_ref, far_ref = refs
    core = lax.rem(lax.axis_index("tensor"), CORES)
    units = blocks[0].shape[0]
    width = near_ref.shape[1]
    for ring, block in enumerate(blocks):
        rows = pl.ds(ring * units, units)
        near_ref[rows, :] = block[:, pl.ds(pl.multiple_of(core * width, 128), width)]
        far_ref[rows, :] = block[:, pl.ds(pl.multiple_of((1 - core) * width, 128), width)]


def down_columns(blocks, width, groups):
    units, rings = blocks[0].shape[0], len(blocks)
    for ring in range(1, rings):
        blocks[ring] = lax.ppermute(
            blocks[ring], "tensor", shift_pairs(groups, ring, 0)
        )
    near, far = pl.pallas_call(
        core_cut_kernel,
        out_shape=[jax.ShapeDtypeStruct((rings * units, width), BF16)] * 2,
        compiler_params=pltpu.CompilerParams(vmem_limit_bytes=VMEM_BYTES),
        name="core_cut",
    )(*[blocks[ring] for ring in range(rings)])
    return near, lax.ppermute(far, "tensor", shift_pairs(groups, 0, 1))


def down_kernel(hidden_ref, near_ref, far_ref, keep_ref, give_ref, held):
    groups, units, _ = hidden_ref.shape
    me = lax.axis_index("tensor")
    for core in range(CORES):
        for ring in range(groups // CORES):
            source = moved_by(me, groups, ring, core, sign=-1)
            held[core, pl.ds(ring * units, units), :] = hidden_ref[source]
    dims = (((0,), (0,)), ((), ()))
    total = lax.dot_general(held[0], near_ref[...], dims, preferred_element_type=F32)
    total = total + lax.dot_general(held[1], far_ref[...], dims, preferred_element_type=F32)
    peers, slots, width = keep_ref.shape
    half = lax.rem(lax.axis_index("expert"), 2)
    rows = total.astype(BF16).reshape(peers, 2 * slots, width)
    low, high = rows[:, :slots, :], rows[:, slots:, :]
    keep_ref[...] = jnp.where(half == 0, low, high)
    give_ref[...] = jnp.where(half == 0, high, low)


def body(tokens, expert_ids, route_weights, gate_weight, up_weight, down_weight):
    devices_wide = lax.axis_size("expert")
    groups = lax.axis_size("tensor")
    experts = devices_wide // 2
    tok_count, per_token = expert_ids.shape
    width = tokens.shape[1]
    units = gate_weight.shape[1]
    capacity = min(tok_count, tok_count * per_token // experts)
    arrived_count = devices_wide * capacity

    ids = expert_ids.T
    rings, wide = groups // CORES, CORES * width
    gate_up = (gate_weight[0], up_weight[0])
    part = jax.ShapeDtypeStruct((2 * units, wide), BF16)
    whole = pl.BlockSpec(memory_space=pl.ANY)
    packed, across = pl.pallas_call(
        lambda *refs: pack_kernel(2, 2, *refs),
        out_shape=[jax.ShapeDtypeStruct((devices_wide, capacity, width), BF16), part],
        in_specs=[whole] * 4,
        out_specs=[whole] * 2,
        scratch_shapes=[
            pltpu.VMEM(ids.shape, jnp.int32),
            pltpu.VMEM(tokens.shape, BF16),
            pltpu.VMEM((devices_wide, capacity, width), BF16),
            pltpu.VMEM(part.shape, BF16),
            pltpu.SemaphoreType.DMA((2,)),
            pltpu.SemaphoreType.DMA((2,)),
            pltpu.SemaphoreType.DMA((2,)),
        ],
        name="pack",
    )(ids, tokens, *gate_up)
    mix = pl.pallas_call(
        lambda *refs: mix_kernel(capacity, 1, *refs),
        out_shape=jax.ShapeDtypeStruct((experts * capacity, tok_count), F32),
        compiler_params=pltpu.CompilerParams(vmem_limit_bytes=VMEM_BYTES),
        name="mix",
    )(ids, route_weights.T)

    ahead, behind = cut([("up", 1), ("up", 3)], *gate_up, down_weight[0], wide)
    pieces = [("down", ring) for ring in (1, 2, 3)] + [("up", 0), ("down", 0)]
    *down, own, down_own = cut(pieces, *gate_up, down_weight[0], wide)
    blocks = [own, ahead, across, behind]
    for ring in range(1, rings):
        blocks[ring] = lax.ppermute(
            blocks[ring], "tensor", shift_pairs(groups, ring, 0)
        )
    arrived = lax.all_to_all(packed, "expert", 0, 0, tiled=True)
    arrived = arrived.reshape(arrived_count, width)
    down_near, down_far = down_columns([down_own, *down], width, groups)

    partner = lax.ppermute(arrived, "tensor", shift_pairs(groups, 0, 1))
    near = pl.pallas_call(
        near_kernel,
        out_shape=jax.ShapeDtypeStruct((rings, 2 * units, arrived_count), F32),
        compiler_params=pltpu.CompilerParams(vmem_limit_bytes=VMEM_BYTES),
        cost_estimate=pl.CostEstimate(flops=10**9, bytes_accessed=10**6, transcendentals=0),
        name="near",
    )(arrived, *blocks)
    partial = pl.pallas_call(
        far_kernel,
        out_shape=jax.ShapeDtypeStruct((rings, 2 * units, arrived_count), BF16),
        out_specs=whole,
        scratch_shapes=[
            pltpu.VMEM((rings, 2 * units, arrived_count), BF16),
            pltpu.SemaphoreType.DMA((rings,)),
        ],
        compiler_params=pltpu.CompilerParams(vmem_limit_bytes=VMEM_BYTES),
        name="far",
    )(partner, near, *blocks)
    same_core = [list(range(core, groups, CORES)) for core in range(CORES)]
    partial = lax.all_to_all(
        partial, "tensor", 0, 0, axis_index_groups=same_core, tiled=True
    )
    hidden = pl.pallas_call(
        hidden_kernel,
        out_shape=jax.ShapeDtypeStruct((groups, units, arrived_count), BF16),
        compiler_params=pltpu.CompilerParams(vmem_limit_bytes=VMEM_BYTES),
        name="hidden",
    )(partial)
    hidden, mix = lax.optimization_barrier((hidden, mix))
    hidden = lax.all_to_all(hidden, "tensor", 0, 0, tiled=True)
    slots = capacity // 2
    kept, given = pl.pallas_call(
        down_kernel,
        out_shape=[jax.ShapeDtypeStruct((devices_wide, slots, width), BF16)] * 2,
        scratch_shapes=[pltpu.VMEM((2, groups // 2 * units, arrived_count), BF16)],
        compiler_params=pltpu.CompilerParams(vmem_limit_bytes=VMEM_BYTES),
        name="down",
    )(hidden, down_near, down_far)
    pairs = [(i, i + 1 - 2 * (i % 2)) for i in range(devices_wide)]
    taken = lax.ppermute(given, "expert", pairs)
    both = (kept.astype(F32) + taken.astype(F32)).astype(BF16)
    returned = lax.all_to_all(both, "expert", 0, 0, tiled=True)
    returned = returned.reshape(devices_wide * slots, width)
    return pl.pallas_call(
        combine_kernel,
        out_shape=jax.ShapeDtypeStruct((tok_count, width), BF16),
        compiler_params=pltpu.CompilerParams(vmem_limit_bytes=VMEM_BYTES),
        name="combine",
    )(mix, returned)


def solution(mesh):
    placed = (
        P("expert", "tensor"),
        P("expert", None),
        P("expert", None),
        P("expert", "tensor", None),
        P("expert", "tensor", None),
        P("expert", "tensor", None),
    )
    def step(*args):
        return body(*args)

    step = jax.shard_map(
        step, mesh=mesh, in_specs=placed, out_specs=P("expert", "tensor"), check_vma=False
    )
    return step
```

```python
import jax
import jax.numpy as jnp
from jax import lax
from jax.experimental import pallas as pl
from jax.experimental.pallas import tpu as pltpu
from jax.sharding import PartitionSpec as P

F32 = jnp.float32
BF16 = jnp.bfloat16


def slot_onehot(ids, slots, capacity, copies):
    per_token, tok_count = ids.shape
    slot = lax.broadcasted_iota(jnp.int32, (slots, tok_count), 0)
    expert = slot // (capacity * copies)
    hit = jnp.zeros((slots, tok_count), F32)
    for j in range(per_token):
        hit = hit + jnp.where(ids[j : j + 1, :] == expert, 1.0, 0.0)
    row = lax.broadcasted_iota(jnp.int32, (tok_count, tok_count), 0)
    col = lax.broadcasted_iota(jnp.int32, (tok_count, tok_count), 1)
    before = jnp.where(row < col, 1.0, 0.0).astype(BF16)
    earlier = jnp.dot(hit.astype(BF16), before, preferred_element_type=F32)
    rank = (slot % capacity).astype(F32)
    return jnp.where((hit > 0.5) & (earlier == rank), 1.0, 0.0), expert


def pack_kernel(copies, ring, ids_ref, tok_ref, *refs):
    *weights, out_ref, block_ref = refs[:5]
    refs = refs[5:]
    ids, tok, packed, held, taken, given, small = refs
    fetches = [
        pltpu.make_async_copy(ids_ref, ids, small.at[0]),
        pltpu.make_async_copy(tok_ref, tok, small.at[1]),
    ]
    for fetch in fetches:
        fetch.start()
    reads = cut_reads(ring, weights, held, taken)
    peers, capacity, width = packed.shape
    for fetch in fetches:
        fetch.wait()
    select, _ = slot_onehot(ids[...], peers * capacity, capacity, copies)
    rows = jnp.dot(select.astype(BF16), tok[...], preferred_element_type=F32)
    packed[...] = rows.reshape(peers, capacity, width).astype(BF16)
    for read in reads:
        read.wait()
    writes = [
        pltpu.make_async_copy(held, block_ref, given.at[0]),
        pltpu.make_async_copy(packed, out_ref, given.at[1]),
    ]
    for write in writes:
        write.start()
    for write in writes:
        write.wait()


def mix_kernel(capacity, copies, ids_ref, route_ref, mix_ref):
    ids = ids_ref[...]
    route = route_ref[...]
    select, expert = slot_onehot(ids, mix_ref.shape[0], capacity, copies)
    weight = jnp.zeros(select.shape, F32)
    for j in range(ids.shape[0]):
        weight = weight + jnp.where(ids[j : j + 1, :] == expert, route[j : j + 1, :], 0.0)
    mix_ref[...] = select * weight


def combine_kernel(mix_ref, rows_ref, out_ref):
    mix = mix_ref[...]
    high = mix.astype(BF16)
    low = (mix - high.astype(F32)).astype(BF16)
    rows = rows_ref[...]
    dims = (((0,), (0,)), ((), ()))
    total = lax.dot_general(high, rows, dims, preferred_element_type=F32)
    total = total + lax.dot_general(low, rows, dims, preferred_element_type=F32)
    out_ref[...] = total.astype(BF16)


CORES = 2
VMEM_BYTES = 10 * 2**20


def moved_by(index, groups, ring, core, sign=1):
    rings = groups // CORES
    place = lax.rem(index // CORES + sign * ring + rings, rings)
    return place * CORES + lax.rem(lax.rem(index, CORES) + core, CORES)


def shift_pairs(groups, ring, core):
    rings = groups // CORES
    return [
        (i, (i // CORES + ring) % rings * CORES + (i + core) % CORES) for i in range(groups)
    ]


def cut_reads(ring, weights, held, taken):
    wide = held.shape[1]
    units, full = weights[0].shape
    rings = full // wide
    chip = lax.axis_index("tensor") // CORES
    cols = pl.ds(pl.multiple_of(lax.rem(chip + ring, rings) * wide, 128), wide)
    reads = []
    for part, weight in enumerate(weights):
        reads.append(
            pltpu.make_async_copy(
                weight.at[:, cols], held.at[pl.ds(part * units, units), :], taken.at[part]
            )
        )
        reads[-1].start()
    return reads


def cut_kernel(rings, *refs):
    *refs, held, taken, given = refs
    weights, outs = refs[: -len(rings)], refs[-len(rings) :]
    reads = [
        cut_reads(ring, weights, held.at[place], taken.at[place])
        for place, ring in enumerate(rings)
    ]
    writes = []
    for place, out in enumerate(outs):
        for read in reads[place]:
            read.wait()
        writes.append(pltpu.make_async_copy(held.at[place], out, given.at[place]))
        writes[-1].start()
    for write in writes:
        write.wait()


def cut(rings, weights, wide):
    parts = len(weights)
    shape = jax.ShapeDtypeStruct((parts * weights[0].shape[0], wide), BF16)
    whole = pl.BlockSpec(memory_space=pl.ANY)
    return pl.pallas_call(
        lambda *refs: cut_kernel(rings, *refs),
        out_shape=[shape] * len(rings),
        in_specs=[whole] * parts,
        out_specs=[whole] * len(rings),
        scratch_shapes=[
            pltpu.VMEM((len(rings), *shape.shape), BF16),
            pltpu.SemaphoreType.DMA((len(rings), parts)),
            pltpu.SemaphoreType.DMA((len(rings),)),
        ],
        name="cut",
    )(*weights)


def half_product(block_ref, rows_ref, half, rows):
    width = rows_ref.shape[1]
    cols = pl.ds(pl.multiple_of(half * width, 128), width)
    return lax.dot_general(
        block_ref[:rows, cols],
        rows_ref[...],
        (((1,), (1,)), ((), ())),
        preferred_element_type=F32,
    )


def near_kernel(rows_ref, *refs):
    *blocks, out_ref = refs
    chip, core = lax.axis_index("tensor") // CORES, lax.rem(lax.axis_index("tensor"), CORES)
    for ring, block in enumerate(blocks):
        source = lax.rem(chip - ring + len(blocks), len(blocks))
        out_ref[source] = half_product(block, rows_ref, core, out_ref.shape[1])


def far_kernel(rows_ref, near_ref, *refs):
    *blocks, out_ref, held, given = refs
    rings = len(blocks)
    chip, core = lax.axis_index("tensor") // CORES, lax.rem(lax.axis_index("tensor"), CORES)
    writes = []
    for ring, block in enumerate(blocks):
        source = lax.rem(chip - ring + rings, rings)
        total = near_ref[source] + half_product(
            block, rows_ref, 1 - core, near_ref.shape[1]
        )
        held[ring] = total.astype(BF16)
        writes.append(pltpu.make_async_copy(held.at[ring], out_ref.at[source], given.at[ring]))
        writes[-1].start()
    for write in writes:
        write.wait()


def hidden_kernel(partial_ref, out_ref):
    groups, units, _ = out_ref.shape
    act = partial_ref[0].astype(F32)
    for g in range(1, partial_ref.shape[0]):
        act = act + partial_ref[g].astype(F32)
    gate, up = act[:units], act[units:]
    hidden = (jax.nn.silu(gate) * up).astype(BF16)
    for g in range(groups):
        out_ref[g] = hidden


def core_cut_kernel(*refs):
    *blocks, near_ref, far_ref = refs
    core = lax.rem(lax.axis_index("tensor"), CORES)
    units = near_ref.shape[0] // len(blocks)
    width = near_ref.shape[1]
    own, other = pl.multiple_of(core * width, 128), pl.multiple_of((1 - core) * width, 128)
    for ring, block in enumerate(blocks):
        rows = pl.ds(ring * units, units)
        last = pl.ds(block.shape[0] - units, units)
        near_ref[rows, :] = block[last, pl.ds(own, width)]
        far_ref[rows, :] = block[last, pl.ds(other, width)]


def down_columns(blocks, width, groups):
    units, rings = blocks[0].shape[0], len(blocks)
    near, far = pl.pallas_call(
        core_cut_kernel,
        out_shape=[jax.ShapeDtypeStruct((rings * units, width), BF16)] * 2,
        compiler_params=pltpu.CompilerParams(vmem_limit_bytes=VMEM_BYTES),
        name="core_cut",
    )(*[blocks[ring] for ring in range(rings)])
    return near, lax.ppermute(far, "tensor", shift_pairs(groups, 0, 1))


def down_kernel(hidden_ref, near_ref, far_ref, keep_ref, give_ref, held):
    groups, units, _ = hidden_ref.shape
    me = lax.axis_index("tensor")
    for core in range(CORES):
        for ring in range(groups // CORES):
            source = moved_by(me, groups, ring, core, sign=-1)
            held[core, pl.ds(ring * units, units), :] = hidden_ref[source]
    dims = (((0,), (0,)), ((), ()))
    total = lax.dot_general(held[0], near_ref[...], dims, preferred_element_type=F32)
    total = total + lax.dot_general(held[1], far_ref[...], dims, preferred_element_type=F32)
    peers, slots, width = keep_ref.shape
    half = lax.rem(lax.axis_index("expert"), 2)
    rows = total.astype(BF16).reshape(peers, 2, slots, width)
    even, odd = rows[:, 0], rows[:, 1]
    keep_ref[...] = jnp.where(half == 0, even, odd)
    give_ref[...] = jnp.where(half == 0, odd, even)


def body(tokens, expert_ids, route_weights, gate_weight, up_weight, down_weight):
    devices_wide = lax.axis_size("expert")
    groups = lax.axis_size("tensor")
    experts = devices_wide // 2
    tok_count, per_token = expert_ids.shape
    width = tokens.shape[1]
    units = gate_weight.shape[1]
    capacity = min(tok_count, tok_count * per_token // experts)
    arrived_count = devices_wide * capacity

    ids = expert_ids.T
    rings, wide = groups // CORES, CORES * width
    weights = (gate_weight[0], up_weight[0], down_weight[0])
    part = jax.ShapeDtypeStruct((3 * units, wide), BF16)
    whole = pl.BlockSpec(memory_space=pl.ANY)
    packed, across = pl.pallas_call(
        lambda *refs: pack_kernel(2, 2, *refs),
        out_shape=[jax.ShapeDtypeStruct((devices_wide, capacity, width), BF16), part],
        in_specs=[whole] * 5,
        out_specs=[whole] * 2,
        scratch_shapes=[
            pltpu.VMEM(ids.shape, jnp.int32),
            pltpu.VMEM(tokens.shape, BF16),
            pltpu.VMEM((devices_wide, capacity, width), BF16),
            pltpu.VMEM(part.shape, BF16),
            pltpu.SemaphoreType.DMA((3,)),
            pltpu.SemaphoreType.DMA((2,)),
            pltpu.SemaphoreType.DMA((2,)),
        ],
        name="pack",
    )(ids, tokens, *weights)
    mix = pl.pallas_call(
        lambda *refs: mix_kernel(capacity, 1, *refs),
        out_shape=jax.ShapeDtypeStruct((experts * capacity, tok_count), F32),
        compiler_params=pltpu.CompilerParams(vmem_limit_bytes=VMEM_BYTES),
        name="mix",
    )(ids, route_weights.T)

    ahead, behind = cut((1, 3), weights, wide)
    (own,) = cut((0,), weights[:2], wide)
    (own_down,) = cut((0,), weights[2:], wide)
    blocks = [own, ahead, across, behind]
    for ring in range(1, rings):
        blocks[ring] = lax.ppermute(
            blocks[ring], "tensor", shift_pairs(groups, ring, 0)
        )
    arrived = lax.all_to_all(packed, "expert", 0, 0, tiled=True)
    arrived = arrived.reshape(arrived_count, width)
    down_near, down_far = down_columns([own_down, *blocks[1:]], width, groups)

    partner = lax.ppermute(arrived, "tensor", shift_pairs(groups, 0, 1))
    near = pl.pallas_call(
        near_kernel,
        out_shape=jax.ShapeDtypeStruct((rings, 2 * units, arrived_count), F32),
        compiler_params=pltpu.CompilerParams(vmem_limit_bytes=VMEM_BYTES),
        cost_estimate=pl.CostEstimate(flops=10**9, bytes_accessed=10**6, transcendentals=0),
        name="near",
    )(arrived, *blocks)
    partial = pl.pallas_call(
        far_kernel,
        out_shape=jax.ShapeDtypeStruct((rings, 2 * units, arrived_count), BF16),
        out_specs=whole,
        scratch_shapes=[
            pltpu.VMEM((rings, 2 * units, arrived_count), BF16),
            pltpu.SemaphoreType.DMA((rings,)),
        ],
        compiler_params=pltpu.CompilerParams(vmem_limit_bytes=VMEM_BYTES),
        name="far",
    )(partner, near, *blocks)
    same_core = [list(range(core, groups, CORES)) for core in range(CORES)]
    partial = lax.all_to_all(
        partial, "tensor", 0, 0, axis_index_groups=same_core, tiled=True
    )
    hidden = pl.pallas_call(
        hidden_kernel,
        out_shape=jax.ShapeDtypeStruct((groups, units, arrived_count), BF16),
        compiler_params=pltpu.CompilerParams(vmem_limit_bytes=VMEM_BYTES),
        name="hidden",
    )(partial)
    hidden, mix = lax.optimization_barrier((hidden, mix))
    hidden = lax.all_to_all(hidden, "tensor", 0, 0, tiled=True)
    kept, given = pl.pallas_call(
        down_kernel,
        out_shape=[jax.ShapeDtypeStruct((experts, capacity, width), BF16)] * 2,
        scratch_shapes=[pltpu.VMEM((2, groups // 2 * units, arrived_count), BF16)],
        compiler_params=pltpu.CompilerParams(vmem_limit_bytes=VMEM_BYTES),
        name="down",
    )(hidden, down_near, down_far)
    pairs = [(i, i + 1 - 2 * (i % 2)) for i in range(devices_wide)]
    taken = lax.ppermute(given, "expert", pairs)
    both = (kept.astype(F32) + taken.astype(F32)).astype(BF16)
    same_half = [list(range(half, devices_wide, 2)) for half in range(2)]
    returned = lax.all_to_all(
        both, "expert", 0, 0, axis_index_groups=same_half, tiled=True
    )
    returned = returned.reshape(experts * capacity, width)
    return pl.pallas_call(
        combine_kernel,
        out_shape=jax.ShapeDtypeStruct((tok_count, width), BF16),
        compiler_params=pltpu.CompilerParams(vmem_limit_bytes=VMEM_BYTES),
        name="combine",
    )(mix, returned)


def solution(mesh):
    placed = (
        P("expert", "tensor"),
        P("expert", None),
        P("expert", None),
        P("expert", "tensor", None),
        P("expert", "tensor", None),
        P("expert", "tensor", None),
    )
    def step(*args):
        return body(*args)

    step = jax.shard_map(
        step, mesh=mesh, in_specs=placed, out_specs=P("expert", "tensor"), check_vma=False
    )
    return step
```

```python
import jax
import jax.numpy as jnp
from jax import lax
from jax.experimental import pallas as pl
from jax.experimental.pallas import tpu as pltpu
from jax.sharding import PartitionSpec as P

F32 = jnp.float32
BF16 = jnp.bfloat16


def slot_onehot(ids, slots, capacity, copies):
    per_token, tok_count = ids.shape
    slot = lax.broadcasted_iota(jnp.int32, (slots, tok_count), 0)
    expert = slot // (capacity * copies)
    hit = jnp.zeros((slots, tok_count), F32)
    for j in range(per_token):
        hit = hit + jnp.where(ids[j : j + 1, :] == expert, 1.0, 0.0)
    row = lax.broadcasted_iota(jnp.int32, (tok_count, tok_count), 0)
    col = lax.broadcasted_iota(jnp.int32, (tok_count, tok_count), 1)
    before = jnp.where(row < col, 1.0, 0.0).astype(BF16)
    earlier = jnp.dot(hit.astype(BF16), before, preferred_element_type=F32)
    rank = (slot % capacity).astype(F32)
    return jnp.where((hit > 0.5) & (earlier == rank), 1.0, 0.0), expert


def pack_kernel(copies, ring, ids_ref, tok_ref, *refs):
    *weights, out_ref, block_ref = refs[:5]
    refs = refs[5:]
    ids, tok, packed, held, taken, given, small = refs
    fetches = [
        pltpu.make_async_copy(ids_ref, ids, small.at[0]),
        pltpu.make_async_copy(tok_ref, tok, small.at[1]),
    ]
    for fetch in fetches:
        fetch.start()
    reads = cut_reads(ring, weights, held, taken)
    peers, capacity, width = packed.shape
    for fetch in fetches:
        fetch.wait()
    select, _ = slot_onehot(ids[...], peers * capacity, capacity, copies)
    rows = jnp.dot(select.astype(BF16), tok[...], preferred_element_type=F32)
    packed[...] = rows.reshape(peers, capacity, width).astype(BF16)
    for read in reads:
        read.wait()
    writes = [
        pltpu.make_async_copy(held, block_ref, given.at[0]),
        pltpu.make_async_copy(packed, out_ref, given.at[1]),
    ]
    for write in writes:
        write.start()
    for write in writes:
        write.wait()


def mix_kernel(capacity, copies, ids_ref, route_ref, mix_ref):
    ids = ids_ref[...]
    route = route_ref[...]
    select, expert = slot_onehot(ids, mix_ref.shape[0], capacity, copies)
    weight = jnp.zeros(select.shape, F32)
    for j in range(ids.shape[0]):
        weight = weight + jnp.where(ids[j : j + 1, :] == expert, route[j : j + 1, :], 0.0)
    mix_ref[...] = select * weight


def combine_kernel(mix_ref, rows_ref, out_ref):
    mix = mix_ref[...]
    high = mix.astype(BF16)
    low = (mix - high.astype(F32)).astype(BF16)
    rows = rows_ref[...]
    dims = (((0,), (0,)), ((), ()))
    total = lax.dot_general(high, rows, dims, preferred_element_type=F32)
    total = total + lax.dot_general(low, rows, dims, preferred_element_type=F32)
    out_ref[...] = total.astype(BF16)


CORES = 2
VMEM_BYTES = 10 * 2**20


def moved_by(index, groups, ring, core, sign=1):
    rings = groups // CORES
    place = lax.rem(index // CORES + sign * ring + rings, rings)
    return place * CORES + lax.rem(lax.rem(index, CORES) + core, CORES)


def shift_pairs(groups, ring, core):
    rings = groups // CORES
    return [
        (i, (i // CORES + ring) % rings * CORES + (i + core) % CORES) for i in range(groups)
    ]


def cut_reads(ring, weights, held, taken):
    wide = held.shape[1]
    units, full = weights[0].shape
    rings = full // wide
    chip = lax.axis_index("tensor") // CORES
    cols = pl.ds(pl.multiple_of(lax.rem(chip + ring, rings) * wide, 128), wide)
    reads = []
    for part, weight in enumerate(weights):
        reads.append(
            pltpu.make_async_copy(
                weight.at[:, cols], held.at[pl.ds(part * units, units), :], taken.at[part]
            )
        )
        reads[-1].start()
    return reads


def cut_kernel(rings, *refs):
    *refs, held, taken, given = refs
    weights, outs = refs[: -len(rings)], refs[-len(rings) :]
    reads = [
        cut_reads(ring, weights, held.at[place], taken.at[place])
        for place, ring in enumerate(rings)
    ]
    writes = []
    for place, out in enumerate(outs):
        for read in reads[place]:
            read.wait()
        writes.append(pltpu.make_async_copy(held.at[place], out, given.at[place]))
        writes[-1].start()
    for write in writes:
        write.wait()


def cut(rings, weights, wide):
    parts = len(weights)
    shape = jax.ShapeDtypeStruct((parts * weights[0].shape[0], wide), BF16)
    whole = pl.BlockSpec(memory_space=pl.ANY)
    return pl.pallas_call(
        lambda *refs: cut_kernel(rings, *refs),
        out_shape=[shape] * len(rings),
        in_specs=[whole] * parts,
        out_specs=[whole] * len(rings),
        scratch_shapes=[
            pltpu.VMEM((len(rings), *shape.shape), BF16),
            pltpu.SemaphoreType.DMA((len(rings), parts)),
            pltpu.SemaphoreType.DMA((len(rings),)),
        ],
        name="cut",
    )(*weights)


def half_product(block_ref, rows_ref, half, rows):
    width = rows_ref.shape[1]
    cols = pl.ds(pl.multiple_of(half * width, 128), width)
    return lax.dot_general(
        block_ref[:rows, cols],
        rows_ref[...],
        (((1,), (1,)), ((), ())),
        preferred_element_type=F32,
    )


def near_kernel(rows_ref, *refs):
    *blocks, out_ref = refs
    chip, core = lax.axis_index("tensor") // CORES, lax.rem(lax.axis_index("tensor"), CORES)
    for ring, block in enumerate(blocks):
        source = lax.rem(chip - ring + len(blocks), len(blocks))
        out_ref[source] = half_product(block, rows_ref, core, out_ref.shape[1])


def far_kernel(rows_ref, near_ref, *refs):
    *blocks, out_ref, held, given = refs
    rings = len(blocks)
    chip, core = lax.axis_index("tensor") // CORES, lax.rem(lax.axis_index("tensor"), CORES)
    writes = []
    for ring, block in enumerate(blocks):
        source = lax.rem(chip - ring + rings, rings)
        total = near_ref[source] + half_product(
            block, rows_ref, 1 - core, near_ref.shape[1]
        )
        held[ring] = total.astype(BF16)
        writes.append(pltpu.make_async_copy(held.at[ring], out_ref.at[source], given.at[ring]))
        writes[-1].start()
    for write in writes:
        write.wait()


def hidden_kernel(partial_ref, out_ref):
    groups, units, _ = out_ref.shape
    act = partial_ref[0].astype(F32)
    for g in range(1, partial_ref.shape[0]):
        act = act + partial_ref[g].astype(F32)
    gate, up = act[:units], act[units:]
    hidden = (jax.nn.silu(gate) * up).astype(BF16)
    for g in range(groups):
        out_ref[g] = hidden


def core_cut_kernel(*refs):
    *blocks, near_ref, far_ref = refs
    core = lax.rem(lax.axis_index("tensor"), CORES)
    units = near_ref.shape[0] // len(blocks)
    width = near_ref.shape[1]
    own, other = pl.multiple_of(core * width, 128), pl.multiple_of((1 - core) * width, 128)
    for ring, block in enumerate(blocks):
        rows = pl.ds(ring * units, units)
        last = pl.ds(block.shape[0] - units, units)
        near_ref[rows, :] = block[last, pl.ds(own, width)]
        far_ref[rows, :] = block[last, pl.ds(other, width)]


def down_columns(blocks, width, groups):
    units, rings = blocks[0].shape[0], len(blocks)
    near, far = pl.pallas_call(
        core_cut_kernel,
        out_shape=[jax.ShapeDtypeStruct((rings * units, width), BF16)] * 2,
        compiler_params=pltpu.CompilerParams(vmem_limit_bytes=VMEM_BYTES),
        name="core_cut",
    )(*[blocks[ring] for ring in range(rings)])
    return near, lax.ppermute(far, "tensor", shift_pairs(groups, 0, 1))


def down_kernel(hidden_ref, near_ref, far_ref, keep_ref, give_ref, held):
    groups, units, _ = hidden_ref.shape
    me = lax.axis_index("tensor")
    for core in range(CORES):
        for ring in range(groups // CORES):
            source = moved_by(me, groups, ring, core, sign=-1)
            held[core, pl.ds(ring * units, units), :] = hidden_ref[source]
    dims = (((0,), (0,)), ((), ()))
    total = lax.dot_general(held[0], near_ref[...], dims, preferred_element_type=F32)
    total = total + lax.dot_general(held[1], far_ref[...], dims, preferred_element_type=F32)
    rows = total.astype(BF16)
    kept = rows.shape[0] // 2
    keep_ref[...] = rows[:kept].reshape(keep_ref.shape)
    give_ref[...] = rows[kept:].reshape(give_ref.shape)


def body(tokens, expert_ids, route_weights, gate_weight, up_weight, down_weight):
    devices_wide = lax.axis_size("expert")
    groups = lax.axis_size("tensor")
    experts = devices_wide // 2
    tok_count, per_token = expert_ids.shape
    width = tokens.shape[1]
    units = gate_weight.shape[1]
    capacity = min(tok_count, tok_count * per_token // experts)
    arrived_count = devices_wide * capacity

    ids = expert_ids.T
    rings, wide = groups // CORES, CORES * width
    weights = (gate_weight[0], up_weight[0], down_weight[0])
    part = jax.ShapeDtypeStruct((3 * units, wide), BF16)
    whole = pl.BlockSpec(memory_space=pl.ANY)
    packed, across = pl.pallas_call(
        lambda *refs: pack_kernel(1, 2, *refs),
        out_shape=[jax.ShapeDtypeStruct((experts, capacity, width), BF16), part],
        in_specs=[whole] * 5,
        out_specs=[whole] * 2,
        scratch_shapes=[
            pltpu.VMEM(ids.shape, jnp.int32),
            pltpu.VMEM(tokens.shape, BF16),
            pltpu.VMEM((experts, capacity, width), BF16),
            pltpu.VMEM(part.shape, BF16),
            pltpu.SemaphoreType.DMA((3,)),
            pltpu.SemaphoreType.DMA((2,)),
            pltpu.SemaphoreType.DMA((2,)),
        ],
        name="pack",
    )(ids, tokens, *weights)
    mix = pl.pallas_call(
        lambda *refs: mix_kernel(capacity, 1, *refs),
        out_shape=jax.ShapeDtypeStruct((experts * capacity, tok_count), F32),
        compiler_params=pltpu.CompilerParams(vmem_limit_bytes=VMEM_BYTES),
        name="mix",
    )(ids, route_weights.T)

    ahead, behind = cut((1, 3), weights[:2], wide)
    (own,) = cut((0,), weights[:2], wide)
    down_ahead, down_behind, own_down = cut((1, 3, 0), weights[2:], wide)
    blocks = [own, ahead, across, behind]
    for ring in range(1, rings):
        blocks[ring] = lax.ppermute(
            blocks[ring], "tensor", shift_pairs(groups, ring, 0)
        )
    down_ahead = lax.ppermute(down_ahead, "tensor", shift_pairs(groups, 1, 0))
    down_behind = lax.ppermute(down_behind, "tensor", shift_pairs(groups, 3, 0))
    same_half = [list(range(half, devices_wide, 2)) for half in range(2)]
    pairs = [(i, i + 1 - 2 * (i % 2)) for i in range(devices_wide)]
    arrived = lax.all_to_all(
        packed, "expert", 0, 0, axis_index_groups=same_half, tiled=True
    )
    arrived = arrived.reshape(experts * capacity, width)
    theirs = lax.ppermute(arrived, "expert", pairs)
    arrived = jnp.concatenate([arrived, theirs], axis=0)
    down_near, down_far = down_columns(
        [own_down, down_ahead, blocks[2], down_behind], width, groups
    )

    partner = lax.ppermute(arrived, "tensor", shift_pairs(groups, 0, 1))
    near = pl.pallas_call(
        near_kernel,
        out_shape=jax.ShapeDtypeStruct((rings, 2 * units, arrived_count), F32),
        compiler_params=pltpu.CompilerParams(vmem_limit_bytes=VMEM_BYTES),
        cost_estimate=pl.CostEstimate(flops=10**9, bytes_accessed=10**6, transcendentals=0),
        name="near",
    )(arrived, *blocks)
    partial = pl.pallas_call(
        far_kernel,
        out_shape=jax.ShapeDtypeStruct((rings, 2 * units, arrived_count), BF16),
        out_specs=whole,
        scratch_shapes=[
            pltpu.VMEM((rings, 2 * units, arrived_count), BF16),
            pltpu.SemaphoreType.DMA((rings,)),
        ],
        compiler_params=pltpu.CompilerParams(vmem_limit_bytes=VMEM_BYTES),
        name="far",
    )(partner, near, *blocks)
    same_core = [list(range(core, groups, CORES)) for core in range(CORES)]
    partial = lax.all_to_all(
        partial, "tensor", 0, 0, axis_index_groups=same_core, tiled=True
    )
    hidden = pl.pallas_call(
        hidden_kernel,
        out_shape=jax.ShapeDtypeStruct((groups, units, arrived_count), BF16),
        compiler_params=pltpu.CompilerParams(vmem_limit_bytes=VMEM_BYTES),
        name="hidden",
    )(partial)
    hidden, mix = lax.optimization_barrier((hidden, mix))
    hidden = lax.all_to_all(hidden, "tensor", 0, 0, tiled=True)
    kept, given = pl.pallas_call(
        down_kernel,
        out_shape=[jax.ShapeDtypeStruct((experts, capacity, width), BF16)] * 2,
        scratch_shapes=[pltpu.VMEM((2, groups // 2 * units, arrived_count), BF16)],
        compiler_params=pltpu.CompilerParams(vmem_limit_bytes=VMEM_BYTES),
        name="down",
    )(hidden, down_near, down_far)
    taken = lax.ppermute(given, "expert", pairs)
    both = (kept.astype(F32) + taken.astype(F32)).astype(BF16)
    returned = lax.all_to_all(
        both, "expert", 0, 0, axis_index_groups=same_half, tiled=True
    )
    returned = returned.reshape(experts * capacity, width)
    return pl.pallas_call(
        combine_kernel,
        out_shape=jax.ShapeDtypeStruct((tok_count, width), BF16),
        compiler_params=pltpu.CompilerParams(vmem_limit_bytes=VMEM_BYTES),
        name="combine",
    )(mix, returned)


def solution(mesh):
    placed = (
        P("expert", "tensor"),
        P("expert", None),
        P("expert", None),
        P("expert", "tensor", None),
        P("expert", "tensor", None),
        P("expert", "tensor", None),
    )
    def step(*args):
        return body(*args)

    step = jax.shard_map(
        step, mesh=mesh, in_specs=placed, out_specs=P("expert", "tensor"), check_vma=False
    )
    return step
```

```python
import jax
import jax.numpy as jnp
from jax import lax
from jax.experimental import pallas as pl
from jax.experimental.pallas import tpu as pltpu
from jax.sharding import PartitionSpec as P

F32 = jnp.float32
BF16 = jnp.bfloat16


def slot_onehot(ids, slots, capacity, copies):
    per_token, tok_count = ids.shape
    slot = lax.broadcasted_iota(jnp.int32, (slots, tok_count), 0)
    expert = slot // (capacity * copies)
    hit = jnp.zeros((slots, tok_count), F32)
    for j in range(per_token):
        hit = hit + jnp.where(ids[j : j + 1, :] == expert, 1.0, 0.0)
    row = lax.broadcasted_iota(jnp.int32, (tok_count, tok_count), 0)
    col = lax.broadcasted_iota(jnp.int32, (tok_count, tok_count), 1)
    before = jnp.where(row < col, 1.0, 0.0).astype(BF16)
    earlier = jnp.dot(hit.astype(BF16), before, preferred_element_type=F32)
    rank = (slot % capacity).astype(F32)
    return jnp.where((hit > 0.5) & (earlier == rank), 1.0, 0.0), expert


def pack_kernel(copies, ring, ids_ref, tok_ref, *refs):
    *weights, out_ref, block_ref = refs[:5]
    refs = refs[5:]
    ids, tok, packed, held, taken, given, small = refs
    fetches = [
        pltpu.make_async_copy(ids_ref, ids, small.at[0]),
        pltpu.make_async_copy(tok_ref, tok, small.at[1]),
    ]
    for fetch in fetches:
        fetch.start()
    reads = cut_reads(ring, weights, held, taken)
    peers, capacity, width = packed.shape
    for fetch in fetches:
        fetch.wait()
    select, _ = slot_onehot(ids[...], peers * capacity, capacity, copies)
    rows = jnp.dot(select.astype(BF16), tok[...], preferred_element_type=F32)
    packed[...] = rows.astype(BF16).reshape(peers, capacity, width)
    for read in reads:
        read.wait()
    writes = [
        pltpu.make_async_copy(held, block_ref, given.at[0]),
        pltpu.make_async_copy(packed, out_ref, given.at[1]),
    ]
    for write in writes:
        write.start()
    for write in writes:
        write.wait()


def mix_kernel(capacity, copies, ids_ref, route_ref, mix_ref):
    ids = ids_ref[...]
    route = route_ref[...]
    select, expert = slot_onehot(ids, mix_ref.shape[0], capacity, copies)
    weight = jnp.zeros(select.shape, F32)
    for j in range(ids.shape[0]):
        weight = weight + jnp.where(ids[j : j + 1, :] == expert, route[j : j + 1, :], 0.0)
    mix_ref[...] = select * weight


def combine_kernel(mix_ref, rows_ref, out_ref):
    mix = mix_ref[...]
    high = mix.astype(BF16)
    low = (mix - high.astype(F32)).astype(BF16)
    rows = rows_ref[...]
    dims = (((0,), (0,)), ((), ()))
    total = lax.dot_general(high, rows, dims, preferred_element_type=F32)
    total = total + lax.dot_general(low, rows, dims, preferred_element_type=F32)
    out_ref[...] = total.astype(BF16)


CORES = 2
VMEM_BYTES = 10 * 2**20


def moved_by(index, groups, ring, core, sign=1):
    rings = groups // CORES
    place = lax.rem(index // CORES + sign * ring + rings, rings)
    return place * CORES + lax.rem(lax.rem(index, CORES) + core, CORES)


def shift_pairs(groups, ring, core):
    rings = groups // CORES
    return [
        (i, (i // CORES + ring) % rings * CORES + (i + core) % CORES) for i in range(groups)
    ]


def cut_reads(ring, weights, held, taken):
    wide = held.shape[1]
    units, full = weights[0].shape
    rings = full // wide
    chip = lax.axis_index("tensor") // CORES
    cols = pl.ds(pl.multiple_of(lax.rem(chip + ring, rings) * wide, 128), wide)
    reads = []
    for part, weight in enumerate(weights):
        reads.append(
            pltpu.make_async_copy(
                weight.at[:, cols], held.at[pl.ds(part * units, units), :], taken.at[part]
            )
        )
        reads[-1].start()
    return reads


def cut_kernel(rings, *refs):
    *refs, held, taken, given = refs
    weights, outs = refs[: -len(rings)], refs[-len(rings) :]
    reads = [
        cut_reads(ring, weights, held.at[place], taken.at[place])
        for place, ring in enumerate(rings)
    ]
    writes = []
    for place, out in enumerate(outs):
        for read in reads[place]:
            read.wait()
        writes.append(pltpu.make_async_copy(held.at[place], out, given.at[place]))
        writes[-1].start()
    for write in writes:
        write.wait()


def cut(rings, weights, wide):
    parts = len(weights)
    shape = jax.ShapeDtypeStruct((parts * weights[0].shape[0], wide), BF16)
    whole = pl.BlockSpec(memory_space=pl.ANY)
    return pl.pallas_call(
        lambda *refs: cut_kernel(rings, *refs),
        out_shape=[shape] * len(rings),
        in_specs=[whole] * parts,
        out_specs=[whole] * len(rings),
        scratch_shapes=[
            pltpu.VMEM((len(rings), *shape.shape), BF16),
            pltpu.SemaphoreType.DMA((len(rings), parts)),
            pltpu.SemaphoreType.DMA((len(rings),)),
        ],
        name="cut",
    )(*weights)


def half_product(block_ref, rows_ref, half, rows):
    width = rows_ref.shape[1]
    cols = pl.ds(pl.multiple_of(half * width, 128), width)
    return lax.dot_general(
        block_ref[:rows, cols],
        rows_ref[...],
        (((1,), (1,)), ((), ())),
        preferred_element_type=F32,
    )


def near_kernel(rows_ref, *refs):
    *blocks, out_ref = refs
    chip, core = lax.axis_index("tensor") // CORES, lax.rem(lax.axis_index("tensor"), CORES)
    for ring, block in enumerate(blocks):
        source = lax.rem(chip - ring + len(blocks), len(blocks))
        out_ref[source] = half_product(block, rows_ref, core, out_ref.shape[1])


def far_kernel(rows_ref, near_ref, *refs):
    *blocks, out_ref, held, given = refs
    rings = len(blocks)
    chip, core = lax.axis_index("tensor") // CORES, lax.rem(lax.axis_index("tensor"), CORES)
    writes = []
    for ring, block in enumerate(blocks):
        source = lax.rem(chip - ring + rings, rings)
        total = near_ref[source] + half_product(
            block, rows_ref, 1 - core, near_ref.shape[1]
        )
        held[ring] = total.astype(BF16)
        writes.append(pltpu.make_async_copy(held.at[ring], out_ref.at[source], given.at[ring]))
        writes[-1].start()
    for write in writes:
        write.wait()


def hidden_kernel(partial_ref, out_ref):
    groups, units, _ = out_ref.shape
    act = partial_ref[0].astype(F32)
    for g in range(1, partial_ref.shape[0]):
        act = act + partial_ref[g].astype(F32)
    gate, up = act[:units], act[units:]
    hidden = (jax.nn.silu(gate) * up).astype(BF16)
    for g in range(groups):
        out_ref[g] = hidden


def core_cut_kernel(*refs):
    *blocks, near_ref, far_ref = refs
    core = lax.rem(lax.axis_index("tensor"), CORES)
    units = near_ref.shape[0] // len(blocks)
    width = near_ref.shape[1]
    own, other = pl.multiple_of(core * width, 128), pl.multiple_of((1 - core) * width, 128)
    for ring, block in enumerate(blocks):
        rows = pl.ds(ring * units, units)
        last = pl.ds(block.shape[0] - units, units)
        near_ref[rows, :] = block[last, pl.ds(own, width)]
        far_ref[rows, :] = block[last, pl.ds(other, width)]


def down_columns(blocks, width, groups):
    units, rings = blocks[0].shape[0], len(blocks)
    near, far = pl.pallas_call(
        core_cut_kernel,
        out_shape=[jax.ShapeDtypeStruct((rings * units, width), BF16)] * 2,
        compiler_params=pltpu.CompilerParams(vmem_limit_bytes=VMEM_BYTES),
        name="core_cut",
    )(*[blocks[ring] for ring in range(rings)])
    return near, lax.ppermute(far, "tensor", shift_pairs(groups, 0, 1))


def down_kernel(other, hidden_ref, near_ref, far_ref, out_ref, held):
    groups, units, count = hidden_ref.shape
    me = lax.axis_index("tensor")
    parity = lax.rem(lax.axis_index("expert") + other, 2)
    rows = pl.ds(pl.multiple_of(parity * (count // 2), 128), count // 2)
    for core in range(CORES):
        for ring in range(groups // CORES):
            source = moved_by(me, groups, ring, core, sign=-1)
            held[core, pl.ds(ring * units, units), :] = hidden_ref[source, :, rows]
    dims = (((0,), (0,)), ((), ()))
    total = lax.dot_general(held[0], near_ref[...], dims, preferred_element_type=F32)
    total = total + lax.dot_general(held[1], far_ref[...], dims, preferred_element_type=F32)
    out_ref[...] = total.astype(BF16).reshape(out_ref.shape)


def body(tokens, expert_ids, route_weights, gate_weight, up_weight, down_weight):
    devices_wide = lax.axis_size("expert")
    groups = lax.axis_size("tensor")
    experts = devices_wide // 2
    tok_count, per_token = expert_ids.shape
    width = tokens.shape[1]
    units = gate_weight.shape[1]
    capacity = min(tok_count, tok_count * per_token // experts)
    arrived_count = devices_wide * capacity

    ids = expert_ids.T
    rings, wide = groups // CORES, CORES * width
    weights = (gate_weight[0], up_weight[0], down_weight[0])
    part = jax.ShapeDtypeStruct((3 * units, wide), BF16)
    whole = pl.BlockSpec(memory_space=pl.ANY)
    packed, across = pl.pallas_call(
        lambda *refs: pack_kernel(2, 2, *refs),
        out_shape=[jax.ShapeDtypeStruct((devices_wide, capacity, width), BF16), part],
        in_specs=[whole] * 5,
        out_specs=[whole] * 2,
        scratch_shapes=[
            pltpu.VMEM(ids.shape, jnp.int32),
            pltpu.VMEM(tokens.shape, BF16),
            pltpu.VMEM((devices_wide, capacity, width), BF16),
            pltpu.VMEM(part.shape, BF16),
            pltpu.SemaphoreType.DMA((3,)),
            pltpu.SemaphoreType.DMA((2,)),
            pltpu.SemaphoreType.DMA((2,)),
        ],
        name="pack",
    )(ids, tokens, *weights)
    mix = pl.pallas_call(
        lambda *refs: mix_kernel(capacity, 1, *refs),
        out_shape=jax.ShapeDtypeStruct((experts * capacity, tok_count), F32),
        compiler_params=pltpu.CompilerParams(vmem_limit_bytes=VMEM_BYTES),
        name="mix",
    )(ids, route_weights.T)

    ahead, behind = cut((1, 3), weights, wide)
    (own,) = cut((0,), weights[:2], wide)
    (own_down,) = cut((0,), weights[2:], wide)
    blocks = [own, ahead, across, behind]
    for ring in range(1, rings):
        blocks[ring] = lax.ppermute(
            blocks[ring], "tensor", shift_pairs(groups, ring, 0)
        )
    arrived = lax.all_to_all(packed, "expert", 0, 0, tiled=True)
    arrived = arrived.reshape(experts, 2, capacity, width)
    arrived = jnp.swapaxes(arrived, 0, 1).reshape(arrived_count, width)
    down_near, down_far = down_columns([own_down, *blocks[1:]], width, groups)

    partner = lax.ppermute(arrived, "tensor", shift_pairs(groups, 0, 1))
    near = pl.pallas_call(
        near_kernel,
        out_shape=jax.ShapeDtypeStruct((rings, 2 * units, arrived_count), F32),
        compiler_params=pltpu.CompilerParams(vmem_limit_bytes=VMEM_BYTES),
        cost_estimate=pl.CostEstimate(flops=10**9, bytes_accessed=10**6, transcendentals=0),
        name="near",
    )(arrived, *blocks)
    partial = pl.pallas_call(
        far_kernel,
        out_shape=jax.ShapeDtypeStruct((rings, 2 * units, arrived_count), BF16),
        out_specs=whole,
        scratch_shapes=[
            pltpu.VMEM((rings, 2 * units, arrived_count), BF16),
            pltpu.SemaphoreType.DMA((rings,)),
        ],
        compiler_params=pltpu.CompilerParams(vmem_limit_bytes=VMEM_BYTES),
        name="far",
    )(partner, near, *blocks)
    same_core = [list(range(core, groups, CORES)) for core in range(CORES)]
    partial = lax.all_to_all(
        partial, "tensor", 0, 0, axis_index_groups=same_core, tiled=True
    )
    hidden = pl.pallas_call(
        hidden_kernel,
        out_shape=jax.ShapeDtypeStruct((groups, units, arrived_count), BF16),
        compiler_params=pltpu.CompilerParams(vmem_limit_bytes=VMEM_BYTES),
        name="hidden",
    )(partial)
    hidden, mix = lax.optimization_barrier((hidden, mix))
    hidden = lax.all_to_all(hidden, "tensor", 0, 0, tiled=True)

    def product(other):
        return pl.pallas_call(
            lambda *refs: down_kernel(other, *refs),
            out_shape=jax.ShapeDtypeStruct((experts, capacity, width), BF16),
            scratch_shapes=[pltpu.VMEM((2, rings * units, arrived_count // 2), BF16)],
            compiler_params=pltpu.CompilerParams(vmem_limit_bytes=VMEM_BYTES),
            cost_estimate=pl.CostEstimate(
                flops=10**8, bytes_accessed=10**6, transcendentals=0
            ),
            name="down",
        )(hidden, down_near, down_far)

    pairs = [(i, i + 1 - 2 * (i % 2)) for i in range(devices_wide)]
    taken = lax.ppermute(product(1), "expert", pairs)
    kept = product(0)
    both = (kept.astype(F32) + taken.astype(F32)).astype(BF16)
    same_half = [list(range(half, devices_wide, 2)) for half in range(2)]
    returned = lax.all_to_all(
        both, "expert", 0, 0, axis_index_groups=same_half, tiled=True
    )
    returned = returned.reshape(experts * capacity, width)
    return pl.pallas_call(
        combine_kernel,
        out_shape=jax.ShapeDtypeStruct((tok_count, width), BF16),
        compiler_params=pltpu.CompilerParams(vmem_limit_bytes=VMEM_BYTES),
        name="combine",
    )(mix, returned)


def solution(mesh):
    placed = (
        P("expert", "tensor"),
        P("expert", None),
        P("expert", None),
        P("expert", "tensor", None),
        P("expert", "tensor", None),
        P("expert", "tensor", None),
    )

    def step(*args):
        return body(*args)

    step = jax.shard_map(
        step, mesh=mesh, in_specs=placed, out_specs=P("expert", "tensor"), check_vma=False
    )
    return step
```

```python
import jax
import jax.numpy as jnp
from jax import lax
from jax.experimental import pallas as pl
from jax.experimental.pallas import tpu as pltpu
from jax.sharding import PartitionSpec as P

F32 = jnp.float32
BF16 = jnp.bfloat16


def slot_onehot(ids, slots, capacity, copies):
    per_token, tok_count = ids.shape
    slot = lax.broadcasted_iota(jnp.int32, (slots, tok_count), 0)
    expert = slot // (capacity * copies)
    hit = jnp.zeros((slots, tok_count), F32)
    for j in range(per_token):
        hit = hit + jnp.where(ids[j : j + 1, :] == expert, 1.0, 0.0)
    row = lax.broadcasted_iota(jnp.int32, (tok_count, tok_count), 0)
    col = lax.broadcasted_iota(jnp.int32, (tok_count, tok_count), 1)
    before = jnp.where(row < col, 1.0, 0.0).astype(BF16)
    earlier = jnp.dot(hit.astype(BF16), before, preferred_element_type=F32)
    rank = (slot % capacity).astype(F32)
    return jnp.where((hit > 0.5) & (earlier == rank), 1.0, 0.0), expert


def pack_kernel(copies, ring, ids_ref, tok_ref, *refs):
    *weights, out_ref, block_ref = refs[:5]
    refs = refs[5:]
    ids, tok, packed, held, taken, given, small = refs
    fetches = [
        pltpu.make_async_copy(ids_ref, ids, small.at[0]),
        pltpu.make_async_copy(tok_ref, tok, small.at[1]),
    ]
    for fetch in fetches:
        fetch.start()
    reads = cut_reads(ring, weights, held, taken)
    peers, capacity, width = packed.shape
    for fetch in fetches:
        fetch.wait()
    select, _ = slot_onehot(ids[...], peers * capacity, capacity, copies)
    rows = jnp.dot(select.astype(BF16), tok[...], preferred_element_type=F32)
    packed[...] = rows.astype(BF16).reshape(peers, capacity, width)
    for read in reads:
        read.wait()
    writes = [
        pltpu.make_async_copy(held, block_ref, given.at[0]),
        pltpu.make_async_copy(packed, out_ref, given.at[1]),
    ]
    for write in writes:
        write.start()
    for write in writes:
        write.wait()


def mix_kernel(capacity, copies, ids_ref, route_ref, mix_ref):
    ids = ids_ref[...]
    route = route_ref[...]
    select, expert = slot_onehot(ids, mix_ref.shape[0], capacity, copies)
    weight = jnp.zeros(select.shape, F32)
    for j in range(ids.shape[0]):
        weight = weight + jnp.where(ids[j : j + 1, :] == expert, route[j : j + 1, :], 0.0)
    mix_ref[...] = select * weight


def combine_kernel(mix_ref, rows_ref, out_ref):
    mix = mix_ref[...]
    high = mix.astype(BF16)
    low = (mix - high.astype(F32)).astype(BF16)
    rows = rows_ref[...]
    dims = (((0,), (0,)), ((), ()))
    total = lax.dot_general(high, rows, dims, preferred_element_type=F32)
    total = total + lax.dot_general(low, rows, dims, preferred_element_type=F32)
    out_ref[...] = total.astype(BF16)


CORES = 2
VMEM_BYTES = 10 * 2**20


def moved_by(index, groups, ring, core, sign=1):
    rings = groups // CORES
    place = lax.rem(index // CORES + sign * ring + rings, rings)
    return place * CORES + lax.rem(lax.rem(index, CORES) + core, CORES)


def shift_pairs(groups, ring, core):
    rings = groups // CORES
    return [
        (i, (i // CORES + ring) % rings * CORES + (i + core) % CORES) for i in range(groups)
    ]


def cut_reads(ring, weights, held, taken):
    wide = held.shape[1]
    units, full = weights[0].shape
    rings = full // wide
    chip = lax.axis_index("tensor") // CORES
    cols = pl.ds(pl.multiple_of(lax.rem(chip + ring, rings) * wide, 128), wide)
    reads = []
    for part, weight in enumerate(weights):
        reads.append(
            pltpu.make_async_copy(
                weight.at[:, cols], held.at[pl.ds(part * units, units), :], taken.at[part]
            )
        )
        reads[-1].start()
    return reads


def cut_kernel(rings, *refs):
    *refs, held, taken, given = refs
    weights, outs = refs[: -len(rings)], refs[-len(rings) :]
    reads = [
        cut_reads(ring, weights, held.at[place], taken.at[place])
        for place, ring in enumerate(rings)
    ]
    writes = []
    for place, out in enumerate(outs):
        for read in reads[place]:
            read.wait()
        writes.append(pltpu.make_async_copy(held.at[place], out, given.at[place]))
        writes[-1].start()
    for write in writes:
        write.wait()


def cut(rings, weights, wide):
    parts = len(weights)
    shape = jax.ShapeDtypeStruct((parts * weights[0].shape[0], wide), BF16)
    whole = pl.BlockSpec(memory_space=pl.ANY)
    return pl.pallas_call(
        lambda *refs: cut_kernel(rings, *refs),
        out_shape=[shape] * len(rings),
        in_specs=[whole] * parts,
        out_specs=[whole] * len(rings),
        scratch_shapes=[
            pltpu.VMEM((len(rings), *shape.shape), BF16),
            pltpu.SemaphoreType.DMA((len(rings), parts)),
            pltpu.SemaphoreType.DMA((len(rings),)),
        ],
        name="cut",
    )(*weights)


def half_product(block_ref, rows_ref, half, rows):
    width = rows_ref.shape[1]
    cols = pl.ds(pl.multiple_of(half * width, 128), width)
    return lax.dot_general(
        block_ref[:rows, cols],
        rows_ref[...],
        (((1,), (1,)), ((), ())),
        preferred_element_type=F32,
    )


def near_kernel(rows_ref, *refs):
    *blocks, out_ref = refs
    chip, core = lax.axis_index("tensor") // CORES, lax.rem(lax.axis_index("tensor"), CORES)
    for ring, block in enumerate(blocks):
        source = lax.rem(chip - ring + len(blocks), len(blocks))
        out_ref[source] = half_product(block, rows_ref, core, out_ref.shape[1])


def far_kernel(rows_ref, near_ref, *refs):
    *blocks, out_ref = refs
    chip, core = lax.axis_index("tensor") // CORES, lax.rem(lax.axis_index("tensor"), CORES)
    for ring, block in enumerate(blocks):
        source = lax.rem(chip - ring + len(blocks), len(blocks))
        product = half_product(block, rows_ref, 1 - core, near_ref.shape[1])
        out_ref[source] = (near_ref[source] + product).astype(BF16)


def hidden_kernel(partial_ref, out_ref):
    groups, units, _ = out_ref.shape
    act = partial_ref[0].astype(F32)
    for g in range(1, partial_ref.shape[0]):
        act = act + partial_ref[g].astype(F32)
    gate, up = act[:units], act[units:]
    hidden = (jax.nn.silu(gate) * up).astype(BF16)
    for g in range(groups):
        out_ref[g] = hidden


def core_cut_kernel(*refs):
    *blocks, near_ref, far_ref = refs
    core = lax.rem(lax.axis_index("tensor"), CORES)
    units = near_ref.shape[0] // len(blocks)
    width = near_ref.shape[1]
    own, other = pl.multiple_of(core * width, 128), pl.multiple_of((1 - core) * width, 128)
    for ring, block in enumerate(blocks):
        rows = pl.ds(ring * units, units)
        last = pl.ds(block.shape[0] - units, units)
        near_ref[rows, :] = block[last, pl.ds(own, width)]
        far_ref[rows, :] = block[last, pl.ds(other, width)]


def down_columns(blocks, width, groups):
    units, rings = blocks[0].shape[0], len(blocks)
    near, far = pl.pallas_call(
        core_cut_kernel,
        out_shape=[jax.ShapeDtypeStruct((rings * units, width), BF16)] * 2,
        compiler_params=pltpu.CompilerParams(vmem_limit_bytes=VMEM_BYTES),
        name="core_cut",
    )(*[blocks[ring] for ring in range(rings)])
    return near, lax.ppermute(far, "tensor", shift_pairs(groups, 0, 1))


def down_kernel(other, hidden_ref, near_ref, far_ref, out_ref, held):
    groups, units, count = hidden_ref.shape
    me = lax.axis_index("tensor")
    parity = lax.rem(lax.axis_index("expert") + other, 2)
    rows = pl.ds(pl.multiple_of(parity * (count // 2), 128), count // 2)
    for core in range(CORES):
        for ring in range(groups // CORES):
            source = moved_by(me, groups, ring, core, sign=-1)
            held[core, pl.ds(ring * units, units), :] = hidden_ref[source, :, rows]
    dims = (((0,), (0,)), ((), ()))
    total = lax.dot_general(held[0], near_ref[...], dims, preferred_element_type=F32)
    total = total + lax.dot_general(held[1], far_ref[...], dims, preferred_element_type=F32)
    out_ref[...] = total.astype(BF16).reshape(out_ref.shape)


def body(tokens, expert_ids, route_weights, gate_weight, up_weight, down_weight):
    devices_wide = lax.axis_size("expert")
    groups = lax.axis_size("tensor")
    experts = devices_wide // 2
    tok_count, per_token = expert_ids.shape
    width = tokens.shape[1]
    units = gate_weight.shape[1]
    capacity = min(tok_count, tok_count * per_token // experts)
    arrived_count = devices_wide * capacity

    ids = expert_ids.T
    rings, wide = groups // CORES, CORES * width
    weights = (gate_weight[0], up_weight[0], down_weight[0])
    part = jax.ShapeDtypeStruct((3 * units, wide), BF16)
    whole = pl.BlockSpec(memory_space=pl.ANY)
    packed, across = pl.pallas_call(
        lambda *refs: pack_kernel(2, 2, *refs),
        out_shape=[jax.ShapeDtypeStruct((devices_wide, capacity, width), BF16), part],
        in_specs=[whole] * 5,
        out_specs=[whole] * 2,
        scratch_shapes=[
            pltpu.VMEM(ids.shape, jnp.int32),
            pltpu.VMEM(tokens.shape, BF16),
            pltpu.VMEM((devices_wide, capacity, width), BF16),
            pltpu.VMEM(part.shape, BF16),
            pltpu.SemaphoreType.DMA((3,)),
            pltpu.SemaphoreType.DMA((2,)),
            pltpu.SemaphoreType.DMA((2,)),
        ],
        name="pack",
    )(ids, tokens, *weights)
    mix = pl.pallas_call(
        lambda *refs: mix_kernel(capacity, 1, *refs),
        out_shape=jax.ShapeDtypeStruct((experts * capacity, tok_count), F32),
        compiler_params=pltpu.CompilerParams(vmem_limit_bytes=VMEM_BYTES),
        name="mix",
    )(ids, route_weights.T)

    ahead, behind = cut((1, 3), weights, wide)
    (own,) = cut((0,), weights[:2], wide)
    (own_down,) = cut((0,), weights[2:], wide)
    blocks = [own, ahead, across, behind]
    for ring in range(1, rings):
        blocks[ring] = lax.ppermute(
            blocks[ring], "tensor", shift_pairs(groups, ring, 0)
        )
    arrived = lax.all_to_all(packed, "expert", 0, 0, tiled=True)
    arrived = arrived.reshape(experts, 2, capacity, width)
    arrived = jnp.swapaxes(arrived, 0, 1).reshape(arrived_count, width)
    down_near, down_far = down_columns([own_down, *blocks[1:]], width, groups)

    arrived, mix = lax.optimization_barrier((arrived, mix))
    partner = lax.ppermute(arrived, "tensor", shift_pairs(groups, 0, 1))
    near = pl.pallas_call(
        near_kernel,
        out_shape=jax.ShapeDtypeStruct((rings, 2 * units, arrived_count), F32),
        compiler_params=pltpu.CompilerParams(vmem_limit_bytes=VMEM_BYTES),
        cost_estimate=pl.CostEstimate(flops=10**9, bytes_accessed=10**6, transcendentals=0),
        name="near",
    )(arrived, *blocks)
    partial = pl.pallas_call(
        far_kernel,
        out_shape=jax.ShapeDtypeStruct((rings, 2 * units, arrived_count), BF16),
        compiler_params=pltpu.CompilerParams(vmem_limit_bytes=VMEM_BYTES),
        name="far",
    )(partner, near, *blocks)
    same_core = [list(range(core, groups, CORES)) for core in range(CORES)]
    partial = lax.all_to_all(
        partial, "tensor", 0, 0, axis_index_groups=same_core, tiled=True
    )
    hidden = pl.pallas_call(
        hidden_kernel,
        out_shape=jax.ShapeDtypeStruct((groups, units, arrived_count), BF16),
        compiler_params=pltpu.CompilerParams(vmem_limit_bytes=VMEM_BYTES),
        name="hidden",
    )(partial)
    hidden = lax.all_to_all(hidden, "tensor", 0, 0, tiled=True)

    def product(other):
        return pl.pallas_call(
            lambda *refs: down_kernel(other, *refs),
            out_shape=jax.ShapeDtypeStruct((experts, capacity, width), BF16),
            scratch_shapes=[pltpu.VMEM((2, rings * units, arrived_count // 2), BF16)],
            compiler_params=pltpu.CompilerParams(vmem_limit_bytes=VMEM_BYTES),
            cost_estimate=pl.CostEstimate(
                flops=10**8, bytes_accessed=10**6, transcendentals=0
            ),
            name="down",
        )(hidden, down_near, down_far)

    pairs = [(i, i + 1 - 2 * (i % 2)) for i in range(devices_wide)]
    taken = lax.ppermute(product(1), "expert", pairs)
    kept = product(0)
    both = (kept.astype(F32) + taken.astype(F32)).astype(BF16)
    same_half = [list(range(half, devices_wide, 2)) for half in range(2)]
    returned = lax.all_to_all(
        both, "expert", 0, 0, axis_index_groups=same_half, tiled=True
    )
    returned = returned.reshape(experts * capacity, width)
    return pl.pallas_call(
        combine_kernel,
        out_shape=jax.ShapeDtypeStruct((tok_count, width), BF16),
        compiler_params=pltpu.CompilerParams(vmem_limit_bytes=VMEM_BYTES),
        name="combine",
    )(mix, returned)


def solution(mesh):
    placed = (
        P("expert", "tensor"),
        P("expert", None),
        P("expert", None),
        P("expert", "tensor", None),
        P("expert", "tensor", None),
        P("expert", "tensor", None),
    )

    def step(*args):
        return body(*args)

    step = jax.shard_map(
        step, mesh=mesh, in_specs=placed, out_specs=P("expert", "tensor"), check_vma=False
    )
    return step
```
